256 devices in a mesh: fsdp: 32 (over x_lo, z, core), proto: 4 (over y), dp: 2 (over x_hi).
Axes of the slice: x: 4 (x_hi: 2, x_lo: 2; x = x_hi * 2 + x_lo), y: 4, z: 8, core: 2. Of those that a mesh axis runs over, the one named last changes fastest.
Arguments:
- teacher_weight: float32 [192, 65536], P(None, ('proto', 'fsdp')), may hold values from -0.4375 to 0.4375
- student_weight: float32 [192, 65536], P(None, ('proto', 'fsdp')), may hold values from -0.4375 to 0.4375
- teacher_feats: bfloat16 [2, 8192, 192], P('dp', 'fsdp'), may hold values from -6 to 6
- student_feats: bfloat16 [2, 8192, 192], P('dp', 'fsdp'), may hold values from -6 to 6
- pairing: int32 [2, 8192], P('dp', 'fsdp'), may hold values from 0 to 255
- center: float32 [65536], P('proto'), may hold values from -10.3 to -3.7
Outputs:
- teacher_new: float32 [192, 65536], P(None, ('proto', 'fsdp'))
- student_grad: float32 [192, 65536], P(None, ('proto', 'fsdp', 'dp'))
The draws below stay inside these ranges and needn't reach their ends.
Inputs may be any that keep to these rules, and one draw needn't show every extreme that they name: pairing[v, r] indexes a crop of the other view in the same block of 256 crops.
All inputs are finite; a program needn't handle non-finite values.
Results may differ from the reference program's by a relative error of at most 0.012.
Values may be sent and summed in bfloat16 or wider, within the bound.
A program may use at most 128 MiB of HBM per device.

```python
import jax
import jax.numpy as jnp
from jax import lax

BOT = 192
PROTO = 65536
CROP_DEV = 256
CROPS = 8192


def draw_center(key, part):
    key_shift = jax.random.fold_in(key, 11)
    key_rough = jax.random.fold_in(key, 12)
    shift = jax.random.uniform(key_shift, (), jnp.float32, 4.0, 6.0)
    rough = jnp.clip(0.05 * jax.random.normal(key_rough, (PROTO,), jnp.float32), -0.3, 0.3)
    return (rough - shift).astype(jnp.float32)


def with_ends(entries, stream_key, low, top_value):
    spot = [jax.random.randint(jax.random.fold_in(stream_key, axis), (), 0, length) for axis, length in enumerate(entries.shape)]
    longest = entries.shape.index(max(entries.shape))
    next_to = spot[:longest] + [(spot[longest] + 1) % entries.shape[longest]] + spot[longest + 1:]
    return entries.at[tuple(spot)].set(low).at[tuple(next_to)].set(top_value)


def block_levels(own_key, extent, cuts, low, high):
    factor_of, own = 1.0, jax.random.fold_in(own_key, 6)
    for axis_at, parts in cuts:
        steps = jnp.exp(jax.random.uniform(jax.random.fold_in(own, axis_at), (parts,), jnp.float32, low / len(cuts), high / len(cuts)))
        factor_of = factor_of * jnp.repeat(steps, extent[axis_at] // parts).reshape([-1 if axis == axis_at else 1 for axis in range(len(extent))])
    return factor_of


def scatter_about(rng, extent, spread, reach, cuts=(), kind=jnp.bfloat16):
    loudness = block_levels(rng, extent, cuts, -0.22, 0.18) if cuts else 1.0
    values = jax.random.normal(rng, extent, jnp.float32) * spread * loudness
    return jnp.minimum(jnp.maximum(values, -reach), reach).astype(kind)


def setup_inputs(seed: int = 0) -> dict:
    streams_of = jax.random.split(jax.random.key(seed), 7)
    teacher_weight = scatter_about(streams_of[0], (BOT, PROTO), BOT ** -0.5, 0.4375, ((1, 128),), jnp.float32)
    student_weight = scatter_about(streams_of[1], (BOT, PROTO), BOT ** -0.5, 0.4375, ((1, 128),), jnp.float32)
    teacher_feats = scatter_about(streams_of[2], (2, CROPS, BOT), 1.0, 6.0, ((0, 2), (1, 32)))
    student_feats = scatter_about(streams_of[3], (2, CROPS, BOT), 1.0, 6.0, ((0, 2), (1, 32)))
    pairing = with_ends(jax.random.randint(streams_of[4], (2, CROPS), 0, CROP_DEV), jax.random.fold_in(streams_of[4], 1), 0, CROP_DEV - 1).astype(jnp.int32)
    center = draw_center(jax.random.fold_in(streams_of[6], 71), 0)
    return {"teacher_weight": teacher_weight, "student_weight": student_weight, "teacher_feats": teacher_feats, "student_feats": student_feats, "pairing": pairing, "center": center}


def normalize_cols(weights):
    return weights * lax.rsqrt(lax.optimization_barrier(jnp.sum(weights * weights, axis=0, keepdims=True)) + 1e-06)

def normalize_rows(feats):
    values = feats.astype(jnp.float32)
    return values * lax.rsqrt(lax.optimization_barrier(jnp.sum(values * values, axis=-1, keepdims=True)) + 1e-06)

def reference(teacher_weight, student_weight, teacher_feats, student_feats, pairing, center):
    teacher_new = 0.994 * teacher_weight + 0.006 * student_weight
    w_teacher = normalize_cols(teacher_new).astype(jnp.bfloat16)
    w_student = normalize_cols(student_weight).astype(jnp.bfloat16)
    z_teacher = normalize_rows(teacher_feats).astype(jnp.bfloat16)
    z_student = normalize_rows(student_feats).astype(jnp.bfloat16)
    base = jnp.arange(CROPS, dtype=jnp.int32) // CROP_DEV * CROP_DEV
    index = (base[None, :] + pairing).astype(jnp.int32)
    other = z_teacher[::-1]
    paired = jax.vmap(lambda table, rows: jnp.take(table, rows, axis=0))(other, index)
    total_rows = 2 * CROPS
    block = 2 * CROP_DEV
    paired_blocks = paired.reshape(total_rows // block, block, BOT)
    student_blocks = z_student.reshape(total_rows // block, block, BOT)

    def step(grad_sum, pieces):
        zp, zs = pieces
        scores_t = (jnp.dot(zp, w_teacher, preferred_element_type=jnp.float32) - center[None, :]) / 0.04
        probs_t = jax.nn.softmax(scores_t, axis=-1)
        scores_s = jnp.dot(zs, w_student, preferred_element_type=jnp.float32) / 0.1
        probs_s = jax.nn.softmax(scores_s, axis=-1)
        derivs = ((probs_s - probs_t) / 0.1).astype(jnp.bfloat16)
        grad_sum = grad_sum + jnp.dot(zs.T, derivs, preferred_element_type=jnp.float32)
        return (grad_sum, None)
    start = jnp.zeros((BOT, PROTO), jnp.float32)
    grad_sum, _ = lax.scan(step, start, (paired_blocks, student_blocks))
    norms = jnp.sqrt(lax.optimization_barrier(jnp.sum(student_weight * student_weight, axis=0, keepdims=True)) + 1e-06)
    unit = student_weight / norms
    student_grad = (grad_sum - unit * lax.optimization_barrier(jnp.sum(unit * grad_sum, axis=0, keepdims=True))) / norms
    return (teacher_new, student_grad)
```

```python
import math

import jax
import jax.numpy as jnp
import numpy as np
from jax import lax
from jax.experimental import pallas as pl
from jax.experimental.pallas import tpu as pltpu
from jax.sharding import PartitionSpec as P

MESH = pl.DeviceIdType.MESH
F32, BF16 = jnp.float32, jnp.bfloat16
T_SCALE = math.log2(math.e) / 0.04
S_SCALE = math.log2(math.e) / 0.1
EPS = 1e-06


def rem(a, n):
    return lax.rem(a, np.int32(n))


def div(a, n):
    return lax.div(a, np.int32(n))


def device(x, y, z, core):
    return ((rem(x, 2) * 8 + z) * 2 + core, y, div(x, 2))


NAMES = (
    ["wr", "wl", "wr2", "wl2"]
    + [f"ws{i}" for i in range(4)]
    + ["cr", "cl", "c2", "pair"]
    + ["sr1", "sl1", "sr2", "sl2"]
    + [f"sx{w}{j}" for w in ("r", "l", "rr", "ll") for j in range(4)]
    + ["txr", "txl", "txrr", "txll"]
    + [f"tz{w}{j}" for w in ("r1", "l1", "r2", "l2") for j in range(4)]
    + [f"x{t}{i}" for t in range(2) for i in range(3)]
    + [f"z{t}{i}" for t in range(2) for i in range(7)]
    + [f"g{i}" for i in range(4)]
    + ["ra", "rb", "rr", "rl"]
)
INDEX = {name: i for i, name in enumerate(NAMES)}


def kernel(
    tw_ref, sw_ref, tf_ref, sf_ref, pair_ref, cen_ref, tnew_ref, grad_ref,
    wbuf, cbuf, zs, zt, ztl, pair_in, e_buf, cb, tot, xin, xsum, zin, at, g, gs_out, gs_in, ry_out, ra_in, ry_in,
    ssem, rsem,
):
    f, y, d = lax.axis_index("fsdp"), lax.axis_index("proto"), lax.axis_index("dp")
    core, z = rem(f, 2), rem(div(f, 2), 8)
    x = d * 2 + div(f, 16)
    parity, chunk = div(y, 2), rem(y, 2)
    away = rem(z + 8 - parity, 8)
    q0 = div(away, 2)
    source = rem(away, 2) == 0
    relay = rem(away, 2) == 1

    def at_x(k):
        return rem(x + k, 4)

    def at_y(k):
        return rem(y + k, 4)

    def at_z(k):
        return rem(z + k, 8)

    def to_x(k):
        return device(at_x(k), y, z, core)

    def to_y(k):
        return device(x, at_y(k), z, core)

    def to_z(k):
        return device(x, y, at_z(k), core)

    sibling = device(x, y, z, 1 - core)
    quarter = [rem(q0 + k, 4) for k in (0, 1, 3, 2)]
    sent = {"all": [], "source": [], "relay": []}

    def copy(name, src, dst, to):
        i = INDEX[name]
        return pltpu.make_async_remote_copy(
            src_ref=src, dst_ref=dst, send_sem=ssem.at[i], recv_sem=rsem.at[i], device_id=to, device_id_type=MESH
        )

    def send_to(who, name, src, dst, to):
        copy(name, src, dst, to).start()
        sent[who].append((name, src.shape, src.dtype))

    def send(who, name, ref, to):
        send_to(who, name, ref, ref, to)

    def arrived(name, ref):
        copy(name, ref, ref, sibling).wait_recv()

    peers = [sibling] + [to_y(k) for k in (1, 2, 3)] + [to_x(k) for k in (1, 2, 3)] + [to_z(k) for k in range(1, 8)]
    barrier = pltpu.get_barrier_semaphore()
    for peer in peers:
        pl.semaphore_signal(barrier, inc=1, device_id=peer, device_id_type=MESH)

    half = pl.ds(pl.multiple_of(d * 256, 256), 256)
    s_cols = sw_ref[:, half]
    t_cols = 0.994 * tw_ref[:, half] + 0.006 * s_cols
    ws = s_cols * lax.rsqrt(jnp.sum(s_cols * s_cols, axis=0, keepdims=True) + EPS)
    wt = t_cols * lax.rsqrt(jnp.sum(t_cols * t_cols, axis=0, keepdims=True) + EPS)
    wbuf[y, core] = jnp.concatenate([wt, ws], axis=0).T.astype(BF16)

    lowest = jnp.min(jnp.min(cen_ref[...], axis=0, keepdims=True), axis=1, keepdims=True)
    cbuf[y, 4:5, :] = jnp.broadcast_to(lowest, (1, 128))
    for k in range(4):
        row = 4 * (f - core) + 4 * (k // 2) + 2 * d + k % 2
        cbuf[y, k : k + 1, :] = cen_ref[pl.ds(row, 1), :]
    cbuf[y, 5:8, :] = jnp.zeros((3, 128), F32)

    @pl.when(source)
    def _():
        feats = sf_ref[:, pl.ds(pl.multiple_of(chunk * 128, 128), 128)].astype(F32)
        zs[q0, x] = (feats * lax.rsqrt(jnp.sum(feats * feats, axis=0, keepdims=True) + EPS)).astype(BF16)

    pl.semaphore_wait(barrier, len(peers))

    @pl.when(source)
    def _():
        send_to("source", "pair", pair_ref.at[:, pl.ds(pl.multiple_of(chunk * 128, 128), 128)], pair_in, to_x(2))
        send("source", "sr1", zs.at[q0, x], to_z(1))
        send("source", "sl1", zs.at[q0, x], to_z(7))
        send("source", "sxr0", zs.at[q0, x], to_x(1))
        send("source", "sxl0", zs.at[q0, x], to_x(3))

    own_w = wbuf.at[y, core]
    send("all", "wr", own_w, to_y(1))
    send("all", "wl", own_w, to_y(3))
    for k, name in ((1, "cr"), (3, "cl"), (2, "c2")):
        send("all", name, cbuf.at[y], to_y(k))
    send("all", "ws0", own_w, sibling)

    low, high = pl.ds(0, 96), pl.ds(96, 96)

    @pl.when(source)
    def _():
        feats = tf_ref[...].astype(F32)
        ztl[...] = (feats * lax.rsqrt(jnp.sum(feats * feats, axis=0, keepdims=True) + EPS)).astype(BF16)
        arrived("pair", pair_in)
        picked = lax.broadcasted_iota(jnp.int32, (256, 128), 0) == pair_in[...]
        onehot = jnp.where(picked, 1.0, 0.0).astype(BF16)
        zt[q0, at_x(2)] = jnp.dot(ztl[...], onehot, preferred_element_type=F32).astype(BF16)
        mine = zt.at[q0, at_x(2)]
        send("source", "txr", mine, to_x(1))
        send("source", "txl", mine, to_x(3))
        send("source", "tzr10", mine, to_z(1))
        send("source", "tzl10", mine, to_z(7))

    tnew_ref[...] = 0.994 * tw_ref[...] + 0.006 * sw_ref[...]

    def cross(who, j):
        send(who, f"sxr{j}", zs.at[quarter[j], x], to_x(1))
        send(who, f"sxl{j}", zs.at[quarter[j], x], to_x(3))

    @pl.when(relay)
    def _():
        arrived("sr1", zs.at[quarter[0], x])
        send("relay", "sr1", zs.at[quarter[0], x], to_z(1))
        arrived("sl1", zs.at[quarter[1], x])
        send("relay", "sl1", zs.at[quarter[1], x], to_z(7))
        cross("relay", 0)
        cross("relay", 1)

    first, last = pl.ds(0, 128), pl.ds(128, 128)
    arrived("wr", wbuf.at[at_y(3), core])
    send("all", "wr2", wbuf.at[at_y(3), core, first], to_y(1))
    arrived("wl", wbuf.at[at_y(1), core])
    send("all", "wl2", wbuf.at[at_y(1), core, last], to_y(3))
    send("all", "ws1", wbuf.at[at_y(3), core], sibling)
    send("all", "ws2", wbuf.at[at_y(1), core], sibling)

    @pl.when(source)
    def _():
        arrived("sr1", zs.at[quarter[2], x])
        send("source", "sr2", zs.at[quarter[2], x], to_z(1))
        arrived("sl1", zs.at[quarter[1], x])
        send("source", "sl2", zs.at[quarter[1], x], to_z(7))
        cross("source", 1)
        cross("source", 2)
        arrived("txr", zt.at[q0, at_x(1)])
        send("source", "txrr", zt.at[q0, at_x(1), low], to_x(1))
        arrived("txl", zt.at[q0, at_x(3)])
        send("source", "txll", zt.at[q0, at_x(3), high], to_x(3))
        for j, k in ((1, 1), (2, 3)):
            send("source", f"tzr1{j}", zt.at[q0, at_x(k)], to_z(1))
            send("source", f"tzl1{j}", zt.at[q0, at_x(k)], to_z(7))

    @pl.when(relay)
    def _():
        arrived("sr2", zs.at[quarter[2], x])
        send("relay", "sr2", zs.at[quarter[2], x, low], to_z(1))
        arrived("sl2", zs.at[quarter[3], x])
        send("relay", "sl2", zs.at[quarter[3], x, high], to_z(7))
        cross("relay", 2)
        cross("relay", 3)

    @pl.when(source)
    def _():
        arrived("txrr", zt.at[q0, x, low])
        arrived("txll", zt.at[q0, x, high])
        send("source", "tzr13", zt.at[q0, x], to_z(1))
        send("source", "tzl13", zt.at[q0, x], to_z(7))
        arrived("sr2", zs.at[quarter[3], x, low])
        arrived("sl2", zs.at[quarter[3], x, high])
        cross("source", 3)

    opposite = wbuf.at[at_y(2), core]
    arrived("wr2", wbuf.at[at_y(2), core, first])
    arrived("wl2", wbuf.at[at_y(2), core, last])
    send("all", "ws3", opposite, sibling)

    for j in range(4):
        arrived(f"sxr{j}", zs.at[quarter[j], at_x(3)])
        send("all", f"sxrr{j}", zs.at[quarter[j], at_x(3), low], to_x(1))
        arrived(f"sxl{j}", zs.at[quarter[j], at_x(1)])
        send("all", f"sxll{j}", zs.at[quarter[j], at_x(1), high], to_x(3))

    across = [at_x(2), at_x(1), at_x(3), x]

    @pl.when(relay)
    def _():
        for j in range(4):
            arrived(f"tzr1{j}", zt.at[quarter[0], across[j]])
            send("relay", f"tzr1{j}", zt.at[quarter[0], across[j]], to_z(1))
            arrived(f"tzl1{j}", zt.at[quarter[1], across[j]])
            send("relay", f"tzl1{j}", zt.at[quarter[1], across[j]], to_z(7))

    for k, name in ((3, "cr"), (1, "cl"), (2, "c2")):
        arrived(name, cbuf.at[at_y(k)])
    floor = jnp.minimum(
        jnp.minimum(cbuf[0, 4:5, :], cbuf[1, 4:5, :]), jnp.minimum(cbuf[2, 4:5, :], cbuf[3, 4:5, :])
    )
    for k in range(16):
        row = (cbuf[k // 4, k % 4 : k % 4 + 1, :] - floor) * T_SCALE
        cb[k * 128 : (k + 1) * 128, :] = jnp.broadcast_to(row, (128, 128)).T

    for i, k in ((0, 0), (1, 3), (2, 1), (3, 2)):
        arrived(f"ws{i}", wbuf.at[at_y(k), 1 - core])
    for j in range(4):
        arrived(f"sxrr{j}", zs.at[quarter[j], at_x(2), low])
        arrived(f"sxll{j}", zs.at[quarter[j], at_x(2), high])

    def scores(which, q, pair):
        z_ref = zs if which else zt
        rhs = jnp.concatenate([z_ref[q, 2 * pair], z_ref[q, 2 * pair + 1]], axis=1)
        pad = jnp.zeros((64, 256), BF16)
        rhs = jnp.concatenate([pad, rhs] if which else [rhs, pad], axis=0)
        lanes = pl.ds(pl.multiple_of(which * 2048 + q * 512 + pair * 256, 256), 256)
        total = jnp.zeros((8, 256), F32)
        for m in range(8):
            rows = pl.ds(m * 256, 256)
            w = wbuf[m // 2, m % 2, :, which * 128 : which * 128 + 256]
            score = jnp.dot(w, rhs, preferred_element_type=F32)
            if which:
                value = jnp.exp2(score * S_SCALE)
            else:
                shift = cb[rows, :]
                value = jnp.exp2(score * T_SCALE - jnp.concatenate([shift, shift], axis=1))
            e_buf[rows, lanes] = value.astype(BF16)
            total = total + jnp.sum(value.reshape(32, 8, 256), axis=0)
        tot[which, pl.ds(q * 2 + pair, 1), :] = jnp.sum(total, axis=0, keepdims=True)

    def loop(low_i, high_i, body):
        lax.fori_loop(low_i, high_i, lambda i, _: body(i), None)

    def student(i):
        scores(1, div(i, 2), rem(i, 2))

    loop(0, 8, student)

    def first_sum(t):
        for i in range(3):
            send_to("all", f"x{t}{i}", tot.at[t], xin.at[t, i], to_x(i + 1))

    def second_sum(t):
        for i in range(3):
            arrived(f"x{t}{i}", xin.at[t, i])
        xsum[t] = tot[t] + xin[t, 0] + xin[t, 1] + xin[t, 2]
        for i in range(7):
            send_to("all", f"z{t}{i}", xsum.at[t], zin.at[t, i], to_z(i + 1))

    def last_sum(t):
        for i in range(7):
            arrived(f"z{t}{i}", zin.at[t, i])
        whole = xsum[t]
        for i in range(7):
            whole = whole + zin[t, i]
        factor = (10.0 if t else -10.0) / whole
        for i in range(8):
            z2 = jnp.concatenate([zs[i // 2, 2 * (i % 2)], zs[i // 2, 2 * (i % 2) + 1]], axis=1).astype(F32)
            at[t, :, i * 256 : (i + 1) * 256] = (z2 * factor[i : i + 1, :]).astype(BF16)

    first_sum(1)

    @pl.when(source)
    def _():
        for j in range(4):
            arrived(f"tzr1{j}", zt.at[quarter[2], across[j]])
            send("source", f"tzr2{j}", zt.at[quarter[2], across[j]], to_z(1))
            arrived(f"tzl1{j}", zt.at[quarter[1], across[j]])
            send("source", f"tzl2{j}", zt.at[quarter[1], across[j]], to_z(7))

    def teacher(q):
        loop(0, 2, lambda i: scores(0, q, i))

    loop(0, 2, lambda i: teacher(rem(q0 + i, 4)))

    @pl.when(relay)
    def _():
        for j in range(4):
            arrived(f"tzr2{j}", zt.at[quarter[2], across[j]])
            if j < 2:
                send("relay", f"tzr2{j}", zt.at[quarter[2], across[j]], to_z(1))
            arrived(f"tzl2{j}", zt.at[quarter[3], across[j]])
            if j >= 2:
                send("relay", f"tzl2{j}", zt.at[quarter[3], across[j]], to_z(7))

    second_sum(1)
    teacher(quarter[2])

    @pl.when(source)
    def _():
        for j in range(4):
            arrived(f"tzr2{j}" if j < 2 else f"tzl2{j}", zt.at[quarter[3], across[j]])

    teacher(quarter[3])
    first_sum(0)
    last_sum(1)

    def term(t, m):
        return lax.dot_general(
            e_buf[pl.ds(pl.multiple_of(m * 256, 256), 256), t * 2048 : (t + 1) * 2048],
            at[t],
            (((1,), (1,)), ((), ())),
            preferred_element_type=F32,
        )

    def student_term(m):
        g[m] = term(1, m)

    loop(0, 3, student_term)
    second_sum(0)
    loop(3, 8, student_term)
    last_sum(0)

    for i, k in enumerate((2, 1, 3, 0)):
        owner = at_y(k)
        theirs, ours = owner * 2 + 1 - core, owner * 2 + core
        gs_out[i] = g[theirs] + term(0, theirs)
        send_to("all", f"g{i}", gs_out.at[i], gs_in.at[i], sibling)
        part = g[ours] + term(0, ours)
        arrived(f"g{i}", gs_in.at[i])
        part = part + gs_in[i]
        if k == 2:
            ry_out[0] = part.astype(BF16)
            send_to("all", "ra", ry_out.at[0, first], ra_in.at[0], to_y(1))
            send_to("all", "rb", ry_out.at[0, last], ra_in.at[1], to_y(3))
        elif k == 1:
            arrived("ra", ra_in.at[0])
            ry_out[1, 0:128] = (part[0:128] + ra_in[0].astype(F32)).astype(BF16)
            ry_out[1, 128:256] = part[128:256].astype(BF16)
            send_to("all", "rr", ry_out.at[1], ry_in.at[0], to_y(1))
        elif k == 3:
            arrived("rb", ra_in.at[1])
            ry_out[2, 0:128] = part[0:128].astype(BF16)
            ry_out[2, 128:256] = (part[128:256] + ra_in[1].astype(F32)).astype(BF16)
            send_to("all", "rl", ry_out.at[2], ry_in.at[1], to_y(3))
        else:
            arrived("rr", ry_in.at[0])
            arrived("rl", ry_in.at[1])
            part = part + ry_in[0].astype(F32) + ry_in[1].astype(F32)
            whole = jnp.concatenate([part, jnp.zeros((256, 64), F32)], axis=1).T[0:192]
            cols = sw_ref[:, half]
            norms = jnp.sqrt(jnp.sum(cols * cols, axis=0, keepdims=True) + EPS)
            unit = cols / norms
            grad_ref[...] = (whole - unit * jnp.sum(unit * whole, axis=0, keepdims=True)) / norms

    some = [
        zs.at[0, 0], zs.at[0, 0, low], wbuf.at[0, 0], wbuf.at[0, 0, first], cbuf.at[0], pair_in, tot.at[0], gs_out.at[0],
        ry_out.at[0], ra_in.at[0],
    ]
    like = {(ref.shape, ref.dtype): ref for ref in some}

    def all_left(who):
        for name, shape, dtype in sent[who]:
            ref = like[shape, dtype]
            copy(name, ref, ref, sibling).wait_send()

    all_left("all")
    pl.when(source)(lambda: all_left("source"))
    pl.when(relay)(lambda: all_left("relay"))


def shards(teacher_weight, student_weight, teacher_feats, student_feats, pairing, center):
    vmem = pl.BlockSpec(memory_space=pltpu.VMEM)
    return pl.pallas_call(
        kernel,
        out_shape=(jax.ShapeDtypeStruct((192, 512), F32), jax.ShapeDtypeStruct((192, 256), F32)),
        in_specs=[vmem] * 6,
        out_specs=(vmem, vmem),
        scratch_shapes=[
            pltpu.VMEM((4, 2, 256, 384), BF16),
            pltpu.VMEM((4, 8, 128), F32),
            pltpu.VMEM((4, 4, 192, 128), BF16),
            pltpu.VMEM((4, 4, 192, 128), BF16),
            pltpu.VMEM((192, 256), BF16),
            pltpu.VMEM((1, 128), jnp.int32),
            pltpu.VMEM((2048, 4096), BF16),
            pltpu.VMEM((2048, 128), F32),
            pltpu.VMEM((2, 8, 256), F32),
            pltpu.VMEM((2, 3, 8, 256), F32),
            pltpu.VMEM((2, 8, 256), F32),
            pltpu.VMEM((2, 7, 8, 256), F32),
            pltpu.VMEM((2, 192, 2048), BF16),
            pltpu.VMEM((8, 256, 192), F32),
            pltpu.VMEM((4, 256, 192), F32),
            pltpu.VMEM((4, 256, 192), F32),
            pltpu.VMEM((3, 256, 192), BF16),
            pltpu.VMEM((2, 128, 192), BF16),
            pltpu.VMEM((2, 256, 192), BF16),
            pltpu.SemaphoreType.DMA((len(NAMES),)),
            pltpu.SemaphoreType.DMA((len(NAMES),)),
        ],
        compiler_params=pltpu.CompilerParams(
            collective_id=0, has_side_effects=True, vmem_limit_bytes=52 * 1024 * 1024
        ),
    )(
        teacher_weight,
        student_weight,
        teacher_feats[0].T,
        student_feats[0].T,
        pairing,
        center.reshape(128, 128),
    )


def solution(mesh):
    columns = P(None, ("proto", "fsdp"))
    return jax.shard_map(
        shards,
        mesh=mesh,
        in_specs=(columns, columns, P("dp", "fsdp", None), P("dp", "fsdp", None), P("dp", "fsdp"), P("proto")),
        out_specs=(columns, P(None, ("proto", "fsdp", "dp"))),
        check_vma=False,
    )
```

```python
import math

import jax
import jax.numpy as jnp
import numpy as np
from jax import lax
from jax.experimental import pallas as pl
from jax.experimental.pallas import tpu as pltpu
from jax.sharding import PartitionSpec as P

MESH = pl.DeviceIdType.MESH
F32, BF16 = jnp.float32, jnp.bfloat16
T_SCALE = math.log2(math.e) / 0.04
S_SCALE = math.log2(math.e) / 0.1
EPS = 1e-06


def rem(a, n):
    return lax.rem(a, np.int32(n))


def div(a, n):
    return lax.div(a, np.int32(n))


def device(x, y, z, core):
    return ((rem(x, 2) * 8 + z) * 2 + core, y, div(x, 2))


RECV = (
    [f"t{i}" for i in range(8)]
    + [f"s{i}" for i in range(8)]
    + ["wra", "wrb", "wla", "wlb", "wr2", "wl2"]
    + [f"ws{i}" for i in range(4)]
    + [f"c{i}" for i in range(1, 4)]
    + [f"x{i}" for i in range(1, 4)]
    + [f"z{i}" for i in range(1, 8)]
    + [f"g{i}" for i in range(4)]
    + [f"y{i}" for i in range(1, 4)]
)
RECV = {name: i for i, name in enumerate(RECV)}
SENDS = 128
LOADS = 6
ORDER = (0, 2, 6, 1, 7, 3, 5, 4)


def kernel(
    tw_hbm, sw_hbm, tf_hbm, sf_hbm, pair_hbm, cen_hbm, grad_ref, norm_ref,
    tw_ref, sw_ref, tf_ref, sf_ref, pair_ref, cen_ref,
    wbuf, cbuf, zs, zt, e_buf, cb, tot, xin, xsum, zin, factor, ag, at, gs_out, gs_in, ry_out, ry_in,
    ssem, rsem, lsem,
):
    f, y, d = lax.axis_index("fsdp"), lax.axis_index("proto"), lax.axis_index("dp")
    core, z = rem(f, 2), rem(div(f, 2), 8)
    x = d * 2 + div(f, 16)

    xs = [rem(x + k, 4) for k in range(4)]
    ys = [rem(y + k, 4) for k in range(4)]
    rows_z = [rem(z + k, 8) for k in range(8)]
    to_x = [device(xs[k], y, z, core) for k in range(4)]
    to_y = [device(x, ys[k], z, core) for k in range(4)]
    to_z = [device(x, y, rows_z[k], core) for k in range(8)]
    sibling = device(x, y, z, 1 - core)
    turn = rem(z + y + 8 - x, 4)
    at_turn = [turn == k for k in range(4)]

    def here(k, student):
        return at_turn[(-k + (0 if student else 2)) % 4]

    sent = []

    def send(when, name, src, dst, to):
        i = len(sent)
        pltpu.make_async_remote_copy(
            src_ref=src, dst_ref=dst, send_sem=ssem.at[i], recv_sem=rsem.at[RECV[name]], device_id=to, device_id_type=MESH
        ).start()
        sent.append((when, src.shape, src.dtype))

    def arrived(name, ref, offset=0):
        pltpu.make_async_remote_copy(
            src_ref=ref, dst_ref=ref, send_sem=ssem.at[0], recv_sem=rsem.at[RECV[name] + offset],
            device_id=sibling, device_id_type=MESH,
        ).wait_recv()

    peers = [sibling] + [to_y[k] for k in (1, 2, 3)] + [to_x[k] for k in (1, 2, 3)] + [to_z[k] for k in range(1, 8)]
    barrier = pltpu.get_barrier_semaphore()
    for peer in peers:
        pl.semaphore_signal(barrier, inc=1, device_id=peer, device_id_type=MESH)

    loads = [
        pltpu.make_async_copy(src, dst, lsem.at[i])
        for i, (src, dst) in enumerate(
            ((sf_hbm, sf_ref), (tf_hbm, tf_ref), (pair_hbm, pair_ref), (sw_hbm, sw_ref), (tw_hbm, tw_ref), (cen_hbm, cen_ref))
        )
    ]
    for load in loads:
        load.start()

    def normalized(feats_ref):
        feats = feats_ref[...].astype(F32)
        return (feats * lax.rsqrt(jnp.sum(feats * feats, axis=0, keepdims=True) + EPS)).astype(BF16)

    for load in loads[:3]:
        load.wait()

    @pl.when(here(0, True))
    def _():
        zs[z, 0:192] = normalized(sf_ref)
        zs[z, 192:208] = jnp.broadcast_to(pair_ref[...].astype(F32), (16, 256)).astype(BF16)

    @pl.when(here(0, False))
    def _():
        zt[z] = normalized(tf_ref)

    pl.semaphore_wait(barrier, len(peers))

    def block(student, k):
        return (zs if student else zt).at[rows_z[k % 8]]

    def name_of(student, k):
        return ("s" if student else "t") + str(k % 8)

    def along_x(when, student, k, steps=(2, 1, 3)):
        for i in steps:
            send(when, name_of(student, k), block(student, k), block(student, k), to_x[i])

    def along_z(when, student, steps, k=0):
        for i in steps:
            send(when, name_of(student, k - i), block(student, k), block(student, k), to_z[i])

    for student in (True, False):
        mine = here(0, student)

        @pl.when(mine)
        def _(student=student, mine=mine):
            along_x(mine, student, 0)
            along_z(mine, student, (2, 6, 3, 5, 4))

    for load in loads[3:]:
        load.wait()
    half = pl.ds(pl.multiple_of(d * 256, 256), 256)
    s_cols = sw_ref[:, half]
    t_cols = 0.994 * tw_ref[:, half] + 0.006 * s_cols
    ws = s_cols * lax.rsqrt(jnp.sum(s_cols * s_cols, axis=0, keepdims=True) + EPS)
    wt = t_cols * lax.rsqrt(jnp.sum(t_cols * t_cols, axis=0, keepdims=True) + EPS)
    wbuf[y, core] = jnp.concatenate([wt, ws], axis=0).T.astype(BF16)

    lowest = jnp.min(jnp.min(cen_ref[...], axis=0, keepdims=True), axis=1, keepdims=True)
    cbuf[y, 4:5, :] = jnp.broadcast_to(lowest, (1, 128))
    for k in range(4):
        row = 4 * (f - core) + 4 * (k // 2) + 2 * d + k % 2
        cbuf[y, k : k + 1, :] = cen_ref[pl.ds(row, 1), :]
    cbuf[y, 5:8, :] = jnp.zeros((3, 128), F32)

    first, last = pl.ds(0, 128), pl.ds(128, 128)
    own = wbuf.at[y, core]
    for name, part, k in (("wra", first, 1), ("wlb", last, 3), ("wrb", last, 1), ("wla", first, 3)):
        send(None, name, own.at[part], own.at[part], to_y[k])
    for k in (1, 3, 2):
        send(None, f"c{k}", cbuf.at[y], cbuf.at[y], to_y[k])
    send(None, "ws0", own, own, sibling)

    def forward(k):
        for student in (True, False):
            mine = here(k, student)

            @pl.when(mine)
            def _(student=student, mine=mine):
                arrived(name_of(student, k), block(student, k))
                along_x(mine, student, k)

    before, after = wbuf.at[ys[3], core], wbuf.at[ys[1], core]
    opposite = wbuf.at[ys[2], core]
    forward(2)
    forward(6)
    arrived("wra", before.at[first])
    send(None, "wr2", before.at[first], before.at[first], to_y[1])
    arrived("wlb", after.at[last])
    send(None, "wl2", after.at[last], after.at[last], to_y[3])

    forward(3)
    forward(5)
    arrived("wrb", before.at[last])
    send(None, "ws1", before, before, sibling)
    arrived("wla", after.at[first])
    send(None, "ws2", after, after, sibling)
    forward(4)
    for student in (True, False):

        @pl.when(jnp.logical_not(here(0, student)))
        def _(student=student):
            arrived(name_of(student, 0), block(student, 0))

        along_z(None, student, (1, 7))

    arrived("wr2", opposite.at[first])
    arrived("wl2", opposite.at[last])
    send(None, "ws3", opposite, opposite, sibling)

    for k in (1, 2, 3):
        arrived(f"c{k}", cbuf.at[ys[(4 - k) % 4]])
    floor = jnp.minimum(
        jnp.minimum(cbuf[0, 4:5, :], cbuf[1, 4:5, :]), jnp.minimum(cbuf[2, 4:5, :], cbuf[3, 4:5, :])
    )
    for k in range(16):
        row = (cbuf[k // 4, k % 4 : k % 4 + 1, :] - floor) * T_SCALE
        cb[k * 128 : (k + 1) * 128, :] = jnp.broadcast_to(row, (128, 128)).T

    for i, k in ((0, 0), (1, 3), (2, 1), (3, 2)):
        arrived(f"ws{i}", wbuf.at[ys[k], 1 - core])

    def scores(student, row, j):
        pad = jnp.zeros((64, 256), BF16)
        rhs = jnp.concatenate([pad, zs[row, 0:192]] if student else [zt[row], pad], axis=0)
        lanes = pl.ds(pl.multiple_of((2048 if student else 0) + j * 256, 256), 256)
        total = jnp.zeros((8, 256), F32)
        low = 128 if student else 0
        for m in range(8):
            rows = pl.ds(m * 256, 256)
            score = jnp.dot(wbuf[m // 2, m % 2, :, low : low + 256], rhs, preferred_element_type=F32)
            if student:
                value = jnp.exp2(score * S_SCALE)
            else:
                shift = cb[rows, :]
                value = jnp.exp2(score * T_SCALE - jnp.concatenate([shift, shift], axis=1))
            e_buf[rows, lanes] = value.astype(BF16)
            total = total + jnp.sum(value.reshape(32, 8, 256), axis=0)
        tot[1 if student else 0, pl.ds(row, 1), :] = jnp.sum(total, axis=0, keepdims=True)

    def offset(j):
        step = div(j + 1, 2)
        step = jnp.where(step == 1, 2, jnp.where(step == 2, 1, step))
        return jnp.where(rem(j, 2) == 1, step, rem(8 - step, 8))

    def chunk(j, _):
        k = offset(j)
        row = rem(z + k, 8)
        for student in (True, False):
            forwarded = rem(turn + k + (0 if student else 2), 4) == 0
            near = jnp.logical_or(k == 1, k == 7)

            @pl.when(jnp.logical_and(k != 0, jnp.logical_or(near, jnp.logical_not(forwarded))))
            def _(student=student):
                arrived("s0" if student else "t0", (zs if student else zt).at[row], k)

            scores(student, row, j)

    lax.fori_loop(0, 8, chunk, None)

    for i in (2, 1, 3):
        send(None, f"x{i}", tot, xin.at[i - 1], to_x[i])

    def paired(j, _):
        row = rem(z + offset(j), 8)
        names = jnp.broadcast_to(zs[row, 192:193].astype(F32), (256, 256))
        crops = lax.broadcasted_iota(jnp.int32, (256, 256), 0).astype(F32)
        onehot = jnp.where(names == crops, 1.0, 0.0).astype(BF16)
        ag[j] = lax.dot_general(
            zs[row, 0:192], onehot, (((1,), (1,)), ((), ())), preferred_element_type=F32
        )

    lax.fori_loop(0, 8, paired, None)
    for i in (1, 2, 3):
        arrived(f"x{i}", xin.at[i - 1])
    xsum[...] = tot[...] + xin[0] + xin[1] + xin[2]
    for i in (4, 3, 5, 2, 6, 1, 7):
        send(None, f"z{i}", xsum, zin.at[i - 1], to_z[i])
    for i in range(1, 8):
        arrived(f"z{i}", zin.at[i - 1])
    whole = xsum[...]
    for i in range(7):
        whole = whole + zin[i]
    factor[...] = 10.0 / whole
    for j in range(8):
        row = rows_z[ORDER[j]]
        at[:, j * 256 : (j + 1) * 256] = (ag[j] * -factor[0, pl.ds(row, 1), :]).astype(BF16)
        scaled = zs[row, 0:192].astype(F32) * factor[1, pl.ds(row, 1), :]
        at[:, 2048 + j * 256 : 2048 + (j + 1) * 256] = scaled.astype(BF16)

    def term(k, whose):
        m = ys[k] * 2 + whose
        return lax.dot_general(
            e_buf[pl.ds(pl.multiple_of(m * 256, 256), 256), :],
            at[...],
            (((1,), (1,)), ((), ())),
            preferred_element_type=F32,
        )

    def theirs(i, k):
        gs_out[i] = term(k, 1 - core)
        send(None, f"g{i}", gs_out.at[i], gs_in.at[i], sibling)

    def ours(i, k):
        part = term(k, core)
        arrived(f"g{i}", gs_in.at[i])
        part = part + gs_in[i]
        return jnp.concatenate([part, jnp.zeros((256, 64), F32)], axis=1).T[0:192]

    theirs(0, 2)
    theirs(1, 1)
    for i, k in enumerate((2, 1, 3)):
        ry_out[i] = ours(i, k).astype(BF16)
        send(None, f"y{k}", ry_out.at[i], ry_in.at[k - 1], to_y[k])
        if i < 2:
            theirs(i + 2, (3, 0)[i])
    total = ours(3, 0)
    for k in (2, 1, 3):
        arrived(f"y{k}", ry_in.at[k - 1])
        total = total + ry_in[k - 1].astype(F32)
    cols = sw_ref[:, half]
    norms = jnp.sqrt(jnp.sum(cols * cols, axis=0, keepdims=True) + EPS)
    unit = cols / norms
    grad_ref[...] = total - unit * jnp.sum(unit * total, axis=0, keepdims=True)
    norm_ref[...] = norms

    some = [
        zs.at[0], zt.at[0], wbuf.at[0, 0], wbuf.at[0, 0, first], cbuf.at[0], tot, gs_out.at[0],
    ]
    like = {(ref.shape, ref.dtype): ref for ref in some}
    for i, (when, shape, dtype) in enumerate(sent):
        ref = like[shape, dtype]

        def drain(i=i, ref=ref):
            pltpu.make_async_remote_copy(
                src_ref=ref, dst_ref=ref, send_sem=ssem.at[i], recv_sem=rsem.at[0], device_id=sibling, device_id_type=MESH
            ).wait_send()

        if when is None:
            drain()
        else:
            pl.when(when)(drain)


def shards(teacher_weight, student_weight, teacher_feats, student_feats, pairing, center):
    hbm = pl.BlockSpec(memory_space=pltpu.HBM)
    vmem = pl.BlockSpec(memory_space=pltpu.VMEM)
    scaled, norms = pl.pallas_call(
        kernel,
        out_shape=(jax.ShapeDtypeStruct((192, 256), F32), jax.ShapeDtypeStruct((1, 256), F32)),
        in_specs=[hbm] * 6,
        out_specs=(vmem, vmem),
        scratch_shapes=[
            pltpu.VMEM((192, 512), F32),
            pltpu.VMEM((192, 512), F32),
            pltpu.VMEM((192, 256), BF16),
            pltpu.VMEM((192, 256), BF16),
            pltpu.VMEM((1, 256), jnp.int32),
            pltpu.VMEM((128, 128), F32),
            pltpu.VMEM((4, 2, 256, 384), BF16),
            pltpu.VMEM((4, 8, 128), F32),
            pltpu.VMEM((8, 208, 256), BF16),
            pltpu.VMEM((8, 192, 256), BF16),
            pltpu.VMEM((2048, 4096), BF16),
            pltpu.VMEM((2048, 128), F32),
            pltpu.VMEM((2, 8, 256), F32),
            pltpu.VMEM((3, 2, 8, 256), F32),
            pltpu.VMEM((2, 8, 256), F32),
            pltpu.VMEM((7, 2, 8, 256), F32),
            pltpu.VMEM((2, 8, 256), F32),
            pltpu.VMEM((8, 192, 256), F32),
            pltpu.VMEM((192, 4096), BF16),
            pltpu.VMEM((4, 256, 192), F32),
            pltpu.VMEM((4, 256, 192), F32),
            pltpu.VMEM((3, 192, 256), BF16),
            pltpu.VMEM((3, 192, 256), BF16),
            pltpu.SemaphoreType.DMA((SENDS,)),
            pltpu.SemaphoreType.DMA((len(RECV),)),
            pltpu.SemaphoreType.DMA((LOADS,)),
        ],
        compiler_params=pltpu.CompilerParams(
            collective_id=0, has_side_effects=True, vmem_limit_bytes=60 * 1024 * 1024
        ),
    )(
        teacher_weight,
        student_weight,
        teacher_feats[0].T,
        student_feats[0].T,
        pairing,
        center.reshape(128, 128),
    )
    return 0.994 * teacher_weight + 0.006 * student_weight, scaled / norms


def solution(mesh):
    columns = P(None, ("proto", "fsdp"))
    return jax.shard_map(
        shards,
        mesh=mesh,
        in_specs=(columns, columns, P("dp", "fsdp", None), P("dp", "fsdp", None), P("dp", "fsdp"), P("proto")),
        out_specs=(columns, P(None, ("proto", "fsdp", "dp"))),
        check_vma=False,
    )
```

```python
import math

import jax
import jax.numpy as jnp
import numpy as np
from jax import lax
from jax.experimental import pallas as pl
from jax.experimental.pallas import tpu as pltpu
from jax.sharding import PartitionSpec as P

MESH = pl.DeviceIdType.MESH
F32, BF16 = jnp.float32, jnp.bfloat16
T_SCALE = math.log2(math.e) / 0.04
S_SCALE = math.log2(math.e) / 0.1
EPS = 1e-06


def rem(a, n):
    return lax.rem(a, np.int32(n))


def div(a, n):
    return lax.div(a, np.int32(n))


def device(x, y, z, core):
    return ((rem(x, 2) * 8 + z) * 2 + core, y, div(x, 2))


RECV = (
    [f"t{i}" for i in range(8)]
    + [f"s{i}" for i in range(8)]
    + ["wra", "wrb", "wla", "wlb", "wr2", "wl2"]
    + [f"ws{i}" for i in range(4)]
    + [f"c{i}" for i in range(1, 4)]
    + [f"x{t}{i}" for t in range(2) for i in range(1, 4)]
    + [f"z{t}{i}" for t in range(2) for i in range(1, 8)]
    + [f"g{i}" for i in range(4)]
    + [f"y{i}" for i in range(1, 4)]
)
RECV = {name: i for i, name in enumerate(RECV)}
SENDS = 128
LOADS = 6
ORDER = (0, 1, 7, 2, 6, 3, 5, 4)


def kernel(
    tw_hbm, sw_hbm, tf_hbm, sf_hbm, pair_hbm, cen_hbm, grad_ref,
    tw_ref, sw_ref, tf_ref, sf_ref, pair_ref, cen_ref,
    wbuf, cbuf, zs, zt, e_buf, cb, tot, xin, xsum, zin, factor, ag, at, g, gs_out, gs_in, ry_out, ry_in,
    ssem, rsem, lsem,
):
    f, y, d = lax.axis_index("fsdp"), lax.axis_index("proto"), lax.axis_index("dp")
    core, z = rem(f, 2), rem(div(f, 2), 8)
    x = d * 2 + div(f, 16)

    xs = [rem(x + k, 4) for k in range(4)]
    ys = [rem(y + k, 4) for k in range(4)]
    rows_z = [rem(z + k, 8) for k in range(8)]
    to_x = [device(xs[k], y, z, core) for k in range(4)]
    to_y = [device(x, ys[k], z, core) for k in range(4)]
    to_z = [device(x, y, rows_z[k], core) for k in range(8)]
    sibling = device(x, y, z, 1 - core)
    turn = rem(z + y + 8 - x, 4)
    at_turn = [turn == k for k in range(4)]

    def here(k, student):
        return at_turn[(-k + (0 if student else 2)) % 4]

    sent = []

    def send(when, name, src, dst, to):
        i = len(sent)
        pltpu.make_async_remote_copy(
            src_ref=src, dst_ref=dst, send_sem=ssem.at[i], recv_sem=rsem.at[RECV[name]], device_id=to, device_id_type=MESH
        ).start()
        sent.append((when, src.shape, src.dtype))

    def arrived(name, ref, offset=0):
        pltpu.make_async_remote_copy(
            src_ref=ref, dst_ref=ref, send_sem=ssem.at[0], recv_sem=rsem.at[RECV[name] + offset],
            device_id=sibling, device_id_type=MESH,
        ).wait_recv()

    peers = [sibling] + [to_y[k] for k in (1, 2, 3)] + [to_x[k] for k in (1, 2, 3)] + [to_z[k] for k in range(1, 8)]
    barrier = pltpu.get_barrier_semaphore()
    for peer in peers:
        pl.semaphore_signal(barrier, inc=1, device_id=peer, device_id_type=MESH)

    loads = [
        pltpu.make_async_copy(src, dst, lsem.at[i])
        for i, (src, dst) in enumerate(
            ((sf_hbm, sf_ref), (tf_hbm, tf_ref), (pair_hbm, pair_ref), (sw_hbm, sw_ref), (tw_hbm, tw_ref), (cen_hbm, cen_ref))
        )
    ]
    for load in loads:
        load.start()

    def normalized(feats_ref):
        feats = feats_ref[...].astype(F32)
        return (feats * lax.rsqrt(jnp.sum(feats * feats, axis=0, keepdims=True) + EPS)).astype(BF16)

    for load in loads[:3]:
        load.wait()

    @pl.when(here(0, True))
    def _():
        zs[z, 0:192] = normalized(sf_ref)
        zs[z, 192:208] = jnp.broadcast_to(pair_ref[...].astype(F32), (16, 256)).astype(BF16)

    @pl.when(here(0, False))
    def _():
        zt[z] = normalized(tf_ref)

    pl.semaphore_wait(barrier, len(peers))

    def block(student, k):
        return (zs if student else zt).at[rows_z[k % 8]]

    def name_of(student, k):
        return ("s" if student else "t") + str(k % 8)

    def along_x(when, student, k, steps=(2, 1, 3)):
        for i in steps:
            send(when, name_of(student, k), block(student, k), block(student, k), to_x[i])

    def along_z(when, student, steps, k=0):
        for i in steps:
            send(when, name_of(student, k - i), block(student, k), block(student, k), to_z[i])

    for student in (True, False):
        mine = here(0, student)

        @pl.when(mine)
        def _(student=student, mine=mine):
            along_x(mine, student, 0)
            along_z(mine, student, (2, 6, 3, 5, 4))

    for load in loads[3:]:
        load.wait()
    half = pl.ds(pl.multiple_of(d * 256, 256), 256)
    s_cols = sw_ref[:, half]
    t_cols = 0.994 * tw_ref[:, half] + 0.006 * s_cols
    ws = s_cols * lax.rsqrt(jnp.sum(s_cols * s_cols, axis=0, keepdims=True) + EPS)
    wt = t_cols * lax.rsqrt(jnp.sum(t_cols * t_cols, axis=0, keepdims=True) + EPS)
    wbuf[y, core] = jnp.concatenate([wt, ws], axis=0).T.astype(BF16)

    lowest = jnp.min(jnp.min(cen_ref[...], axis=0, keepdims=True), axis=1, keepdims=True)
    cbuf[y, 4:5, :] = jnp.broadcast_to(lowest, (1, 128))
    for k in range(4):
        row = 4 * (f - core) + 4 * (k // 2) + 2 * d + k % 2
        cbuf[y, k : k + 1, :] = cen_ref[pl.ds(row, 1), :]
    cbuf[y, 5:8, :] = jnp.zeros((3, 128), F32)

    first, last = pl.ds(0, 128), pl.ds(128, 128)
    own = wbuf.at[y, core]
    for name, part, k in (("wra", first, 1), ("wlb", last, 3), ("wrb", last, 1), ("wla", first, 3)):
        send(None, name, own.at[part], own.at[part], to_y[k])
    for k in (1, 3, 2):
        send(None, f"c{k}", cbuf.at[y], cbuf.at[y], to_y[k])
    send(None, "ws0", own, own, sibling)

    def forward(k):
        for student in (True, False):
            mine = here(k, student)

            @pl.when(mine)
            def _(student=student, mine=mine):
                arrived(name_of(student, k), block(student, k))
                along_x(mine, student, k)

    before, after = wbuf.at[ys[3], core], wbuf.at[ys[1], core]
    opposite = wbuf.at[ys[2], core]
    forward(2)
    forward(6)
    for student in (True, False):

        @pl.when(jnp.logical_not(here(0, student)))
        def _(student=student):
            arrived(name_of(student, 0), block(student, 0))

        along_z(None, student, (1, 7))

    arrived("wra", before.at[first])
    send(None, "wr2", before.at[first], before.at[first], to_y[1])
    arrived("wlb", after.at[last])
    send(None, "wl2", after.at[last], after.at[last], to_y[3])

    forward(3)
    forward(5)
    arrived("wrb", before.at[last])
    send(None, "ws1", before, before, sibling)
    arrived("wla", after.at[first])
    send(None, "ws2", after, after, sibling)
    forward(4)
    arrived("wr2", opposite.at[first])
    arrived("wl2", opposite.at[last])
    send(None, "ws3", opposite, opposite, sibling)

    for k in (1, 2, 3):
        arrived(f"c{k}", cbuf.at[ys[(4 - k) % 4]])
    floor = jnp.minimum(
        jnp.minimum(cbuf[0, 4:5, :], cbuf[1, 4:5, :]), jnp.minimum(cbuf[2, 4:5, :], cbuf[3, 4:5, :])
    )
    for k in range(16):
        row = (cbuf[k // 4, k % 4 : k % 4 + 1, :] - floor) * T_SCALE
        cb[k * 128 : (k + 1) * 128, :] = jnp.broadcast_to(row, (128, 128)).T

    for i, k in ((0, 0), (1, 3), (2, 1), (3, 2)):
        arrived(f"ws{i}", wbuf.at[ys[k], 1 - core])

    def scores(student, row, j):
        pad = jnp.zeros((64, 256), BF16)
        rhs = jnp.concatenate([pad, zs[row, 0:192]] if student else [zt[row], pad], axis=0)
        lanes = pl.ds(pl.multiple_of((2048 if student else 0) + j * 256, 256), 256)
        total = jnp.zeros((8, 256), F32)
        low = 128 if student else 0
        for m in range(8):
            rows = pl.ds(m * 256, 256)
            score = jnp.dot(wbuf[m // 2, m % 2, :, low : low + 256], rhs, preferred_element_type=F32)
            if student:
                value = jnp.exp2(score * S_SCALE)
            else:
                shift = cb[rows, :]
                value = jnp.exp2(score * T_SCALE - jnp.concatenate([shift, shift], axis=1))
            e_buf[rows, lanes] = value.astype(BF16)
            total = total + jnp.sum(value.reshape(32, 8, 256), axis=0)
        tot[1 if student else 0, pl.ds(row, 1), :] = jnp.sum(total, axis=0, keepdims=True)

    def offset(j):
        step = div(j + 1, 2)
        return jnp.where(rem(j, 2) == 1, step, rem(8 - step, 8))

    def chunk(student):
        def body(j, _):
            k = offset(j)
            row = rem(z + k, 8)
            forwarded = rem(turn + k + (0 if student else 2), 4) == 0
            near = jnp.logical_or(k == 1, k == 7)

            @pl.when(jnp.logical_and(k != 0, jnp.logical_or(near, jnp.logical_not(forwarded))))
            def _():
                arrived("s0" if student else "t0", (zs if student else zt).at[row], k)

            scores(student, row, j)

        return body

    def over_x(t):
        for i in (2, 1, 3):
            send(None, f"x{t}{i}", tot.at[t], xin.at[t, i - 1], to_x[i])

    def over_z(t):
        for i in (1, 2, 3):
            arrived(f"x{t}{i}", xin.at[t, i - 1])
        xsum[t] = tot[t] + xin[t, 0] + xin[t, 1] + xin[t, 2]
        for i in (4, 3, 5, 2, 6, 1, 7):
            send(None, f"z{t}{i}", xsum.at[t], zin.at[t, i - 1], to_z[i])

    def totals(t):
        for i in range(1, 8):
            arrived(f"z{t}{i}", zin.at[t, i - 1])
        whole = xsum[t]
        for i in range(7):
            whole = whole + zin[t, i]
        factor[t] = 10.0 / whole

    lax.fori_loop(0, 8, chunk(True), None)
    over_x(1)
    lax.fori_loop(0, 8, chunk(False), None)
    over_x(0)
    over_z(1)

    def paired(j, _):
        row = rem(z + offset(j), 8)
        names = jnp.broadcast_to(zs[row, 192:193].astype(F32), (256, 256))
        crops = lax.broadcasted_iota(jnp.int32, (256, 256), 0).astype(F32)
        onehot = jnp.where(names == crops, 1.0, 0.0).astype(BF16)
        ag[j] = lax.dot_general(
            zs[row, 0:192], onehot, (((1,), (1,)), ((), ())), preferred_element_type=F32
        )

    lax.fori_loop(0, 8, paired, None)
    over_z(0)
    totals(1)
    for j in range(8):
        row = rows_z[ORDER[j]]
        scaled = zs[row, 0:192].astype(F32) * factor[1, pl.ds(row, 1), :]
        at[1, :, j * 256 : (j + 1) * 256] = scaled.astype(BF16)

    def term(t, m):
        return lax.dot_general(
            e_buf[pl.ds(pl.multiple_of(m * 256, 256), 256), t * 2048 : (t + 1) * 2048],
            at[t],
            (((1,), (1,)), ((), ())),
            preferred_element_type=F32,
        )

    def student_term(m, _):
        g[m] = term(1, m)

    lax.fori_loop(0, 8, student_term, None)
    totals(0)
    for j in range(8):
        row = rows_z[ORDER[j]]
        at[0, :, j * 256 : (j + 1) * 256] = (ag[j] * -factor[0, pl.ds(row, 1), :]).astype(BF16)

    def both(k, whose):
        m = ys[k] * 2 + whose
        return g[m] + term(0, m)

    def theirs(i, k):
        gs_out[i] = both(k, 1 - core)
        send(None, f"g{i}", gs_out.at[i], gs_in.at[i], sibling)

    def ours(i, k):
        part = both(k, core)
        arrived(f"g{i}", gs_in.at[i])
        part = part + gs_in[i]
        return jnp.concatenate([part, jnp.zeros((256, 64), F32)], axis=1).T[0:192]

    theirs(0, 2)
    theirs(1, 1)
    for i, k in enumerate((2, 1, 3)):
        if i == 0:
            theirs(2, 3)
        ry_out[i] = ours(i, k).astype(BF16)
        send(None, f"y{k}", ry_out.at[i], ry_in.at[k - 1], to_y[k])
    theirs(3, 0)
    total = ours(3, 0)
    for k in (2, 1, 3):
        arrived(f"y{k}", ry_in.at[k - 1])
        total = total + ry_in[k - 1].astype(F32)
    cols = sw_ref[:, half]
    norms = jnp.sqrt(jnp.sum(cols * cols, axis=0, keepdims=True) + EPS)
    unit = cols / norms
    grad_ref[...] = (total - unit * jnp.sum(unit * total, axis=0, keepdims=True)) / norms

    some = [
        zs.at[0], zt.at[0], wbuf.at[0, 0], wbuf.at[0, 0, first], cbuf.at[0], tot.at[0], gs_out.at[0],
    ]
    like = {(ref.shape, ref.dtype): ref for ref in some}
    for i, (when, shape, dtype) in enumerate(sent):
        ref = like[shape, dtype]

        def drain(i=i, ref=ref):
            pltpu.make_async_remote_copy(
                src_ref=ref, dst_ref=ref, send_sem=ssem.at[i], recv_sem=rsem.at[0], device_id=sibling, device_id_type=MESH
            ).wait_send()

        if when is None:
            drain()
        else:
            pl.when(when)(drain)


def shards(teacher_weight, student_weight, teacher_feats, student_feats, pairing, center):
    hbm = pl.BlockSpec(memory_space=pltpu.HBM)
    vmem = pl.BlockSpec(memory_space=pltpu.VMEM)
    student_grad = pl.pallas_call(
        kernel,
        out_shape=jax.ShapeDtypeStruct((192, 256), F32),
        in_specs=[hbm] * 6,
        out_specs=vmem,
        scratch_shapes=[
            pltpu.VMEM((192, 512), F32),
            pltpu.VMEM((192, 512), F32),
            pltpu.VMEM((192, 256), BF16),
            pltpu.VMEM((192, 256), BF16),
            pltpu.VMEM((1, 256), jnp.int32),
            pltpu.VMEM((128, 128), F32),
            pltpu.VMEM((4, 2, 256, 384), BF16),
            pltpu.VMEM((4, 8, 128), F32),
            pltpu.VMEM((8, 208, 256), BF16),
            pltpu.VMEM((8, 192, 256), BF16),
            pltpu.VMEM((2048, 4096), BF16),
            pltpu.VMEM((2048, 128), F32),
            pltpu.VMEM((2, 8, 256), F32),
            pltpu.VMEM((2, 3, 8, 256), F32),
            pltpu.VMEM((2, 8, 256), F32),
            pltpu.VMEM((2, 7, 8, 256), F32),
            pltpu.VMEM((2, 8, 256), F32),
            pltpu.VMEM((8, 192, 256), F32),
            pltpu.VMEM((2, 192, 2048), BF16),
            pltpu.VMEM((8, 256, 192), F32),
            pltpu.VMEM((4, 256, 192), F32),
            pltpu.VMEM((4, 256, 192), F32),
            pltpu.VMEM((3, 192, 256), BF16),
            pltpu.VMEM((3, 192, 256), BF16),
            pltpu.SemaphoreType.DMA((SENDS,)),
            pltpu.SemaphoreType.DMA((len(RECV),)),
            pltpu.SemaphoreType.DMA((LOADS,)),
        ],
        compiler_params=pltpu.CompilerParams(
            collective_id=0, has_side_effects=True, vmem_limit_bytes=60 * 1024 * 1024
        ),
    )(
        teacher_weight,
        student_weight,
        teacher_feats[0].T,
        student_feats[0].T,
        pairing,
        center.reshape(128, 128),
    )
    return 0.994 * teacher_weight + 0.006 * student_weight, student_grad


def solution(mesh):
    columns = P(None, ("proto", "fsdp"))
    return jax.shard_map(
        shards,
        mesh=mesh,
        in_specs=(columns, columns, P("dp", "fsdp", None), P("dp", "fsdp", None), P("dp", "fsdp"), P("proto")),
        out_specs=(columns, P(None, ("proto", "fsdp", "dp"))),
        check_vma=False,
    )
```

```python
import math

import jax
import jax.numpy as jnp
import numpy as np
from jax import lax
from jax.experimental import pallas as pl
from jax.experimental.pallas import tpu as pltpu
from jax.sharding import PartitionSpec as P

MESH = pl.DeviceIdType.MESH
F32, BF16 = jnp.float32, jnp.bfloat16
T_SCALE = math.log2(math.e) / 0.04
S_SCALE = math.log2(math.e) / 0.1
EPS = 1e-06


def rem(a, n):
    return lax.rem(a, np.int32(n))


def div(a, n):
    return lax.div(a, np.int32(n))


def device(x, y, z, core):
    return ((rem(x, 2) * 8 + z) * 2 + core, y, div(x, 2))


RECV = (
    [f"t{i}" for i in range(8)]
    + [f"s{i}" for i in range(8)]
    + ["wra", "wrb", "wla", "wlb", "wr2", "wl2"]
    + [f"ws{i}" for i in range(4)]
    + [f"c{i}" for i in range(1, 4)]
    + [f"x{t}{i}" for t in range(2) for i in range(1, 4)]
    + [f"z{t}{i}" for t in range(2) for i in range(1, 8)]
    + [f"g{i}" for i in range(4)]
    + [f"y{i}" for i in range(1, 4)]
)
RECV = {name: i for i, name in enumerate(RECV)}
SENDS = 128
LOADS = 6
ORDER = (0, 1, 7, 2, 6, 3, 5, 4)


def kernel(
    tw_hbm, sw_hbm, tf_hbm, sf_hbm, pair_hbm, cen_hbm, grad_ref,
    tw_ref, sw_ref, tf_ref, sf_ref, pair_ref, cen_ref,
    wbuf, cbuf, zs, zt, e_buf, cb, tot, xin, xsum, zin, factor, ag, at, g, gs_out, gs_in, ry_out, ry_in,
    ssem, rsem, lsem,
):
    f, y, d = lax.axis_index("fsdp"), lax.axis_index("proto"), lax.axis_index("dp")
    core, z = rem(f, 2), rem(div(f, 2), 8)
    x = d * 2 + div(f, 16)

    xs = [rem(x + k, 4) for k in range(4)]
    ys = [rem(y + k, 4) for k in range(4)]
    rows_z = [rem(z + k, 8) for k in range(8)]
    to_x = [device(xs[k], y, z, core) for k in range(4)]
    to_y = [device(x, ys[k], z, core) for k in range(4)]
    to_z = [device(x, y, rows_z[k], core) for k in range(8)]
    sibling = device(x, y, z, 1 - core)
    turn = rem(z + y + 8 - x, 4)
    at_turn = [turn == k for k in range(4)]

    def here(k, student):
        return at_turn[(-k + (0 if student else 2)) % 4]

    sent = []

    def send(when, name, src, dst, to):
        i = len(sent)
        pltpu.make_async_remote_copy(
            src_ref=src, dst_ref=dst, send_sem=ssem.at[i], recv_sem=rsem.at[RECV[name]], device_id=to, device_id_type=MESH
        ).start()
        sent.append((when, src.shape, src.dtype))

    def arrived(name, ref, offset=0):
        pltpu.make_async_remote_copy(
            src_ref=ref, dst_ref=ref, send_sem=ssem.at[0], recv_sem=rsem.at[RECV[name] + offset],
            device_id=sibling, device_id_type=MESH,
        ).wait_recv()

    peers = [sibling] + [to_y[k] for k in (1, 2, 3)] + [to_x[k] for k in (1, 2, 3)] + [to_z[k] for k in range(1, 8)]
    barrier = pltpu.get_barrier_semaphore()
    for peer in peers:
        pl.semaphore_signal(barrier, inc=1, device_id=peer, device_id_type=MESH)

    loads = [
        pltpu.make_async_copy(src, dst, lsem.at[i])
        for i, (src, dst) in enumerate(
            ((sf_hbm, sf_ref), (tf_hbm, tf_ref), (pair_hbm, pair_ref), (sw_hbm, sw_ref), (tw_hbm, tw_ref), (cen_hbm, cen_ref))
        )
    ]
    for load in loads:
        load.start()

    def normalized(feats_ref):
        feats = feats_ref[...].astype(F32)
        return (feats * lax.rsqrt(jnp.sum(feats * feats, axis=0, keepdims=True) + EPS)).astype(BF16)

    for load in loads[:3]:
        load.wait()

    @pl.when(here(0, True))
    def _():
        zs[z, 0:192] = normalized(sf_ref)
        zs[z, 192:208] = jnp.broadcast_to(pair_ref[...].astype(F32), (16, 256)).astype(BF16)

    @pl.when(here(0, False))
    def _():
        zt[z] = normalized(tf_ref)

    pl.semaphore_wait(barrier, len(peers))

    def block(student, k):
        return (zs if student else zt).at[rows_z[k % 8]]

    def name_of(student, k):
        return ("s" if student else "t") + str(k % 8)

    def along_x(when, student, k, steps=(2, 1, 3)):
        for i in steps:
            send(when, name_of(student, k), block(student, k), block(student, k), to_x[i])

    def along_z(when, student, steps, k=0):
        for i in steps:
            send(when, name_of(student, k - i), block(student, k), block(student, k), to_z[i])

    for student in (True, False):
        mine = here(0, student)

        @pl.when(mine)
        def _(student=student, mine=mine):
            along_x(mine, student, 0)
            along_z(mine, student, (2, 6, 3, 5, 4) if student else (2, 6))

    for load in loads[3:]:
        load.wait()
    half = pl.ds(pl.multiple_of(d * 256, 256), 256)
    s_cols = sw_ref[:, half]
    t_cols = 0.994 * tw_ref[:, half] + 0.006 * s_cols
    ws = s_cols * lax.rsqrt(jnp.sum(s_cols * s_cols, axis=0, keepdims=True) + EPS)
    wt = t_cols * lax.rsqrt(jnp.sum(t_cols * t_cols, axis=0, keepdims=True) + EPS)
    wbuf[y, core] = jnp.concatenate([wt, ws], axis=0).T.astype(BF16)

    lowest = jnp.min(jnp.min(cen_ref[...], axis=0, keepdims=True), axis=1, keepdims=True)
    cbuf[y, 4:5, :] = jnp.broadcast_to(lowest, (1, 128))
    for k in range(4):
        row = 4 * (f - core) + 4 * (k // 2) + 2 * d + k % 2
        cbuf[y, k : k + 1, :] = cen_ref[pl.ds(row, 1), :]
    cbuf[y, 5:8, :] = jnp.zeros((3, 128), F32)

    first, last = pl.ds(0, 128), pl.ds(128, 128)
    own = wbuf.at[y, core]
    for name, part, k in (("wra", first, 1), ("wlb", last, 3), ("wrb", last, 1), ("wla", first, 3)):
        send(None, name, own.at[part], own.at[part], to_y[k])
    for k in (1, 3, 2):
        send(None, f"c{k}", cbuf.at[y], cbuf.at[y], to_y[k])
    send(None, "ws0", own, own, sibling)

    def forward(k):
        for student in (True, False):
            mine = here(k, student)

            @pl.when(mine)
            def _(student=student, mine=mine):
                arrived(name_of(student, k), block(student, k))
                if not student and k == 2:
                    along_z(mine, student, (7, 6), k)
                if not student and k == 6:
                    along_z(mine, student, (1,), k)
                along_x(mine, student, k, (2, 1, 3) if student or k == 4 else (3, 1))

    def relay(k):
        mine = here(k - 1, False)

        @pl.when(mine)
        def _():
            arrived(name_of(False, k), block(False, k))
            along_x(mine, False, k, (3,))

    before, after = wbuf.at[ys[3], core], wbuf.at[ys[1], core]
    opposite = wbuf.at[ys[2], core]
    forward(2)
    forward(6)
    for student in (True, False):

        @pl.when(jnp.logical_not(here(0, student)))
        def _(student=student):
            arrived(name_of(student, 0), block(student, 0))

        along_z(None, student, (1, 7))

    arrived("wra", before.at[first])
    send(None, "wr2", before.at[first], before.at[first], to_y[1])
    arrived("wlb", after.at[last])
    send(None, "wl2", after.at[last], after.at[last], to_y[3])

    forward(3)
    forward(5)
    arrived("wrb", before.at[last])
    send(None, "ws1", before, before, sibling)
    arrived("wla", after.at[first])
    send(None, "ws2", after, after, sibling)
    forward(4)
    relay(2)
    relay(6)
    arrived("wr2", opposite.at[first])
    arrived("wl2", opposite.at[last])
    send(None, "ws3", opposite, opposite, sibling)

    for k in (1, 2, 3):
        arrived(f"c{k}", cbuf.at[ys[(4 - k) % 4]])
    floor = jnp.minimum(
        jnp.minimum(cbuf[0, 4:5, :], cbuf[1, 4:5, :]), jnp.minimum(cbuf[2, 4:5, :], cbuf[3, 4:5, :])
    )
    for k in range(16):
        row = (cbuf[k // 4, k % 4 : k % 4 + 1, :] - floor) * T_SCALE
        cb[k * 128 : (k + 1) * 128, :] = jnp.broadcast_to(row, (128, 128)).T

    for i, k in ((0, 0), (1, 3), (2, 1), (3, 2)):
        arrived(f"ws{i}", wbuf.at[ys[k], 1 - core])

    def scores(student, row, j):
        pad = jnp.zeros((64, 256), BF16)
        rhs = jnp.concatenate([pad, zs[row, 0:192]] if student else [zt[row], pad], axis=0)
        lanes = pl.ds(pl.multiple_of((2048 if student else 0) + j * 256, 256), 256)
        total = jnp.zeros((8, 256), F32)
        low = 128 if student else 0
        for m in range(8):
            rows = pl.ds(m * 256, 256)
            score = jnp.dot(wbuf[m // 2, m % 2, :, low : low + 256], rhs, preferred_element_type=F32)
            if student:
                value = jnp.exp2(score * S_SCALE)
            else:
                shift = cb[rows, :]
                value = jnp.exp2(score * T_SCALE - jnp.concatenate([shift, shift], axis=1))
            e_buf[rows, lanes] = value.astype(BF16)
            total = total + jnp.sum(value.reshape(32, 8, 256), axis=0)
        tot[1 if student else 0, pl.ds(row, 1), :] = jnp.sum(total, axis=0, keepdims=True)

    def offset(j):
        step = div(j + 1, 2)
        return jnp.where(rem(j, 2) == 1, step, rem(8 - step, 8))

    def chunk(student):
        def body(j, _):
            k = offset(j)
            row = rem(z + k, 8)
            forwarded = rem(turn + k + (0 if student else 2), 4) == 0
            if not student:
                relayed = jnp.logical_and(rem(turn + k + 1, 4) == 0, k != 4)
                forwarded = jnp.logical_or(forwarded, relayed)
            near = jnp.logical_or(k == 1, k == 7)

            @pl.when(jnp.logical_and(k != 0, jnp.logical_or(near, jnp.logical_not(forwarded))))
            def _():
                arrived("s0" if student else "t0", (zs if student else zt).at[row], k)

            scores(student, row, j)

        return body

    def over_x(t):
        for i in (2, 1, 3):
            send(None, f"x{t}{i}", tot.at[t], xin.at[t, i - 1], to_x[i])

    def over_z(t):
        for i in (1, 2, 3):
            arrived(f"x{t}{i}", xin.at[t, i - 1])
        xsum[t] = tot[t] + xin[t, 0] + xin[t, 1] + xin[t, 2]
        for i in (4, 3, 5, 2, 6, 1, 7):
            send(None, f"z{t}{i}", xsum.at[t], zin.at[t, i - 1], to_z[i])

    def totals(t):
        for i in range(1, 8):
            arrived(f"z{t}{i}", zin.at[t, i - 1])
        whole = xsum[t]
        for i in range(7):
            whole = whole + zin[t, i]
        factor[t] = 10.0 / whole

    lax.fori_loop(0, 5, chunk(True), None)
    relay(3)
    relay(5)
    lax.fori_loop(5, 8, chunk(True), None)
    over_x(1)
    lax.fori_loop(0, 8, chunk(False), None)
    over_x(0)
    over_z(1)

    def paired(j, _):
        row = rem(z + offset(j), 8)
        names = jnp.broadcast_to(zs[row, 192:193].astype(F32), (256, 256))
        crops = lax.broadcasted_iota(jnp.int32, (256, 256), 0).astype(F32)
        onehot = jnp.where(names == crops, 1.0, 0.0).astype(BF16)
        ag[j] = lax.dot_general(
            zs[row, 0:192], onehot, (((1,), (1,)), ((), ())), preferred_element_type=F32
        )

    lax.fori_loop(0, 8, paired, None)
    over_z(0)
    totals(1)
    for j in range(8):
        row = rows_z[ORDER[j]]
        scaled = zs[row, 0:192].astype(F32) * factor[1, pl.ds(row, 1), :]
        at[1, :, j * 256 : (j + 1) * 256] = scaled.astype(BF16)

    def term(t, m):
        return lax.dot_general(
            e_buf[pl.ds(pl.multiple_of(m * 256, 256), 256), t * 2048 : (t + 1) * 2048],
            at[t],
            (((1,), (1,)), ((), ())),
            preferred_element_type=F32,
        )

    def student_term(m, _):
        g[m] = term(1, m)

    lax.fori_loop(0, 8, student_term, None)
    totals(0)
    for j in range(8):
        row = rows_z[ORDER[j]]
        at[0, :, j * 256 : (j + 1) * 256] = (ag[j] * -factor[0, pl.ds(row, 1), :]).astype(BF16)

    def both(k, whose):
        m = ys[k] * 2 + whose
        return g[m] + term(0, m)

    def theirs(i, k):
        gs_out[i] = both(k, 1 - core)
        send(None, f"g{i}", gs_out.at[i], gs_in.at[i], sibling)

    def ours(i, k):
        part = both(k, core)
        arrived(f"g{i}", gs_in.at[i])
        part = part + gs_in[i]
        return jnp.concatenate([part, jnp.zeros((256, 64), F32)], axis=1).T[0:192]

    theirs(0, 2)
    theirs(1, 1)
    for i, k in enumerate((2, 1, 3)):
        if i == 0:
            theirs(2, 3)
        ry_out[i] = ours(i, k).astype(BF16)
        send(None, f"y{k}", ry_out.at[i], ry_in.at[k - 1], to_y[k])
    theirs(3, 0)
    total = ours(3, 0)
    for k in (2, 1, 3):
        arrived(f"y{k}", ry_in.at[k - 1])
        total = total + ry_in[k - 1].astype(F32)
    cols = sw_ref[:, half]
    norms = jnp.sqrt(jnp.sum(cols * cols, axis=0, keepdims=True) + EPS)
    unit = cols / norms
    grad_ref[...] = (total - unit * jnp.sum(unit * total, axis=0, keepdims=True)) / norms

    some = [
        zs.at[0], zt.at[0], wbuf.at[0, 0], wbuf.at[0, 0, first], cbuf.at[0], tot.at[0], gs_out.at[0],
    ]
    like = {(ref.shape, ref.dtype): ref for ref in some}
    for i, (when, shape, dtype) in enumerate(sent):
        ref = like[shape, dtype]

        def drain(i=i, ref=ref):
            pltpu.make_async_remote_copy(
                src_ref=ref, dst_ref=ref, send_sem=ssem.at[i], recv_sem=rsem.at[0], device_id=sibling, device_id_type=MESH
            ).wait_send()

        if when is None:
            drain()
        else:
            pl.when(when)(drain)


def shards(teacher_weight, student_weight, teacher_feats, student_feats, pairing, center):
    hbm = pl.BlockSpec(memory_space=pltpu.HBM)
    vmem = pl.BlockSpec(memory_space=pltpu.VMEM)
    student_grad = pl.pallas_call(
        kernel,
        out_shape=jax.ShapeDtypeStruct((192, 256), F32),
        in_specs=[hbm] * 6,
        out_specs=vmem,
        scratch_shapes=[
            pltpu.VMEM((192, 512), F32),
            pltpu.VMEM((192, 512), F32),
            pltpu.VMEM((192, 256), BF16),
            pltpu.VMEM((192, 256), BF16),
            pltpu.VMEM((1, 256), jnp.int32),
            pltpu.VMEM((128, 128), F32),
            pltpu.VMEM((4, 2, 256, 384), BF16),
            pltpu.VMEM((4, 8, 128), F32),
            pltpu.VMEM((8, 208, 256), BF16),
            pltpu.VMEM((8, 192, 256), BF16),
            pltpu.VMEM((2048, 4096), BF16),
            pltpu.VMEM((2048, 128), F32),
            pltpu.VMEM((2, 8, 256), F32),
            pltpu.VMEM((2, 3, 8, 256), F32),
            pltpu.VMEM((2, 8, 256), F32),
            pltpu.VMEM((2, 7, 8, 256), F32),
            pltpu.VMEM((2, 8, 256), F32),
            pltpu.VMEM((8, 192, 256), F32),
            pltpu.VMEM((2, 192, 2048), BF16),
            pltpu.VMEM((8, 256, 192), F32),
            pltpu.VMEM((4, 256, 192), F32),
            pltpu.VMEM((4, 256, 192), F32),
            pltpu.VMEM((3, 192, 256), BF16),
            pltpu.VMEM((3, 192, 256), BF16),
            pltpu.SemaphoreType.DMA((SENDS,)),
            pltpu.SemaphoreType.DMA((len(RECV),)),
            pltpu.SemaphoreType.DMA((LOADS,)),
        ],
        compiler_params=pltpu.CompilerParams(
            collective_id=0, has_side_effects=True, vmem_limit_bytes=60 * 1024 * 1024
        ),
    )(
        teacher_weight,
        student_weight,
        teacher_feats[0].T,
        student_feats[0].T,
        pairing,
        center.reshape(128, 128),
    )
    return 0.994 * teacher_weight + 0.006 * student_weight, student_grad


def solution(mesh):
    columns = P(None, ("proto", "fsdp"))
    return jax.shard_map(
        shards,
        mesh=mesh,
        in_specs=(columns, columns, P("dp", "fsdp", None), P("dp", "fsdp", None), P("dp", "fsdp"), P("proto")),
        out_specs=(columns, P(None, ("proto", "fsdp", "dp"))),
        check_vma=False,
    )
```

```python
import math

import jax
import jax.numpy as jnp
import numpy as np
from jax import lax
from jax.experimental import pallas as pl
from jax.experimental.pallas import tpu as pltpu
from jax.sharding import PartitionSpec as P

MESH = pl.DeviceIdType.MESH
F32, BF16 = jnp.float32, jnp.bfloat16
T_SCALE = math.log2(math.e) / 0.04
S_SCALE = math.log2(math.e) / 0.1
EPS = 1e-06


def rem(a, n):
    return lax.rem(a, np.int32(n))


def div(a, n):
    return lax.div(a, np.int32(n))


def device(x, y, z, core):
    return ((rem(x, 2) * 8 + z) * 2 + core, y, div(x, 2))


RECV = (
    [f"t{i}" for i in range(8)]
    + [f"s{i}" for i in range(8)]
    + ["wra", "wrb", "wla", "wlb", "wr2", "wl2"]
    + [f"ws{i}" for i in range(4)]
    + [f"c{i}" for i in range(1, 4)]
    + [f"x{t}{i}" for t in range(2) for i in range(1, 4)]
    + [f"z{t}{i}" for t in range(2) for i in range(1, 8)]
    + [f"g{i}" for i in range(4)]
    + [f"y{i}" for i in range(1, 4)]
)
RECV = {name: i for i, name in enumerate(RECV)}
SENDS = 128
LOADS = 6
ORDER = (0, 1, 7, 2, 6, 3, 5, 4)


def kernel(
    tw_hbm, sw_hbm, tf_hbm, sf_hbm, pair_hbm, cen_hbm, grad_ref,
    tw_ref, sw_ref, tf_ref, sf_ref, pair_ref, cen_ref,
    wbuf, cbuf, zs, zt, e_buf, cb, tot, xin, xsum, zin, factor, ag, at, g, gs_out, gs_in, ry_out, ry_in,
    ssem, rsem, lsem,
):
    f, y, d = lax.axis_index("fsdp"), lax.axis_index("proto"), lax.axis_index("dp")
    core, z = rem(f, 2), rem(div(f, 2), 8)
    x = d * 2 + div(f, 16)

    xs = [rem(x + k, 4) for k in range(4)]
    ys = [rem(y + k, 4) for k in range(4)]
    rows_z = [rem(z + k, 8) for k in range(8)]
    to_x = [device(xs[k], y, z, core) for k in range(4)]
    to_y = [device(x, ys[k], z, core) for k in range(4)]
    to_z = [device(x, y, rows_z[k], core) for k in range(8)]
    sibling = device(x, y, z, 1 - core)
    turn = rem(z + y + 8 - x, 4)
    at_turn = [turn == k for k in range(4)]

    def here(k, student):
        return at_turn[(-k + (0 if student else 2)) % 4]

    sent = []

    def send(when, name, src, dst, to):
        i = len(sent)
        pltpu.make_async_remote_copy(
            src_ref=src, dst_ref=dst, send_sem=ssem.at[i], recv_sem=rsem.at[RECV[name]], device_id=to, device_id_type=MESH
        ).start()
        sent.append((when, src.shape, src.dtype))

    def arrived(name, ref, offset=0):
        pltpu.make_async_remote_copy(
            src_ref=ref, dst_ref=ref, send_sem=ssem.at[0], recv_sem=rsem.at[RECV[name] + offset],
            device_id=sibling, device_id_type=MESH,
        ).wait_recv()

    peers = [sibling] + [to_y[k] for k in (1, 2, 3)] + [to_x[k] for k in (1, 2, 3)] + [to_z[k] for k in range(1, 8)]
    barrier = pltpu.get_barrier_semaphore()
    for peer in peers:
        pl.semaphore_signal(barrier, inc=1, device_id=peer, device_id_type=MESH)

    loads = [
        pltpu.make_async_copy(src, dst, lsem.at[i])
        for i, (src, dst) in enumerate(
            ((sf_hbm, sf_ref), (tf_hbm, tf_ref), (pair_hbm, pair_ref), (sw_hbm, sw_ref), (tw_hbm, tw_ref), (cen_hbm, cen_ref))
        )
    ]
    for load in loads:
        load.start()

    def normalized(feats_ref):
        feats = feats_ref[...].astype(F32)
        return (feats * lax.rsqrt(jnp.sum(feats * feats, axis=0, keepdims=True) + EPS)).astype(BF16)

    for load in loads[:3]:
        load.wait()

    @pl.when(here(0, True))
    def _():
        zs[z, 0:192] = normalized(sf_ref)
        zs[z, 192:208] = jnp.broadcast_to(pair_ref[...].astype(F32), (16, 256)).astype(BF16)

    @pl.when(here(0, False))
    def _():
        zt[z] = normalized(tf_ref)

    pl.semaphore_wait(barrier, len(peers))

    def block(student, k):
        return (zs if student else zt).at[rows_z[k % 8]]

    def name_of(student, k):
        return ("s" if student else "t") + str(k % 8)

    def along_x(when, student, k, steps=(2, 1, 3)):
        for i in steps:
            send(when, name_of(student, k), block(student, k), block(student, k), to_x[i])

    def along_z(when, student, steps, k=0):
        for i in steps:
            send(when, name_of(student, k - i), block(student, k), block(student, k), to_z[i])

    for student in (True, False):
        mine = here(0, student)

        @pl.when(mine)
        def _(student=student, mine=mine):
            along_x(mine, student, 0)
            along_z(mine, student, (2, 6))

    for load in loads[3:]:
        load.wait()
    half = pl.ds(pl.multiple_of(d * 256, 256), 256)
    s_cols = sw_ref[:, half]
    t_cols = 0.994 * tw_ref[:, half] + 0.006 * s_cols
    ws = s_cols * lax.rsqrt(jnp.sum(s_cols * s_cols, axis=0, keepdims=True) + EPS)
    wt = t_cols * lax.rsqrt(jnp.sum(t_cols * t_cols, axis=0, keepdims=True) + EPS)
    wbuf[y, core] = jnp.concatenate([wt, ws], axis=0).T.astype(BF16)

    lowest = jnp.min(jnp.min(cen_ref[...], axis=0, keepdims=True), axis=1, keepdims=True)
    cbuf[y, 4:5, :] = jnp.broadcast_to(lowest, (1, 128))
    for k in range(4):
        row = 4 * (f - core) + 4 * (k // 2) + 2 * d + k % 2
        cbuf[y, k : k + 1, :] = cen_ref[pl.ds(row, 1), :]
    cbuf[y, 5:8, :] = jnp.zeros((3, 128), F32)

    first, last = pl.ds(0, 128), pl.ds(128, 128)
    own = wbuf.at[y, core]
    for name, part, k in (("wra", first, 1), ("wlb", last, 3), ("wrb", last, 1), ("wla", first, 3)):
        send(None, name, own.at[part], own.at[part], to_y[k])
    for k in (1, 3, 2):
        send(None, f"c{k}", cbuf.at[y], cbuf.at[y], to_y[k])
    send(None, "ws0", own, own, sibling)

    def forward(k):
        for student in (True, False):
            mine = here(k, student)

            @pl.when(mine)
            def _(student=student, mine=mine):
                arrived(name_of(student, k), block(student, k))
                if k == 2:
                    along_z(mine, student, (7,) if student else (7, 6), k)
                if k == 6:
                    along_z(mine, student, (1, 2) if student else (1,), k)
                along_x(mine, student, k, (2, 1, 3) if student or k == 4 else (3, 1))

    def relay(k):
        mine = here(k - 1, False)

        @pl.when(mine)
        def _():
            arrived(name_of(False, k), block(False, k))
            along_x(mine, False, k, (3,))

    before, after = wbuf.at[ys[3], core], wbuf.at[ys[1], core]
    opposite = wbuf.at[ys[2], core]
    forward(2)
    forward(6)
    for student in (True, False):

        @pl.when(jnp.logical_not(here(0, student)))
        def _(student=student):
            arrived(name_of(student, 0), block(student, 0))

        along_z(None, student, (1, 7))

    arrived("wra", before.at[first])
    send(None, "wr2", before.at[first], before.at[first], to_y[1])
    arrived("wlb", after.at[last])
    send(None, "wl2", after.at[last], after.at[last], to_y[3])

    for k in (1, 2, 3):
        arrived(f"c{k}", cbuf.at[ys[(4 - k) % 4]])
    floor = jnp.minimum(
        jnp.minimum(cbuf[0, 4:5, :], cbuf[1, 4:5, :]), jnp.minimum(cbuf[2, 4:5, :], cbuf[3, 4:5, :])
    )
    for k in range(16):
        row = (cbuf[k // 4, k % 4 : k % 4 + 1, :] - floor) * T_SCALE
        cb[k * 128 : (k + 1) * 128, :] = jnp.broadcast_to(row, (128, 128)).T

    forward(3)
    forward(5)
    arrived("wrb", before.at[last])
    send(None, "ws1", before, before, sibling)
    arrived("wla", after.at[first])
    send(None, "ws2", after, after, sibling)
    forward(4)
    relay(2)
    relay(6)
    arrived("wr2", opposite.at[first])
    arrived("wl2", opposite.at[last])
    send(None, "ws3", opposite, opposite, sibling)

    for i, k in ((0, 0), (1, 3), (2, 1), (3, 2)):
        arrived(f"ws{i}", wbuf.at[ys[k], 1 - core])

    def scores(student, row, j):
        pad = jnp.zeros((64, 256), BF16)
        rhs = jnp.concatenate([pad, zs[row, 0:192]] if student else [zt[row], pad], axis=0)
        lanes = pl.ds(pl.multiple_of((2048 if student else 0) + j * 256, 256), 256)
        total = jnp.zeros((8, 256), F32)
        low = 128 if student else 0
        for m in range(8):
            rows = pl.ds(m * 256, 256)
            score = jnp.dot(wbuf[m // 2, m % 2, :, low : low + 256], rhs, preferred_element_type=F32)
            if student:
                value = jnp.exp2(score * S_SCALE)
            else:
                shift = cb[rows, :]
                value = jnp.exp2(score * T_SCALE - jnp.concatenate([shift, shift], axis=1))
            e_buf[rows, lanes] = value.astype(BF16)
            total = total + jnp.sum(value.reshape(32, 8, 256), axis=0)
        tot[1 if student else 0, pl.ds(row, 1), :] = jnp.sum(total, axis=0, keepdims=True)

    def offset(j):
        step = div(j + 1, 2)
        return jnp.where(rem(j, 2) == 1, step, rem(8 - step, 8))

    def chunk(student):
        def body(j, _):
            k = offset(j)
            row = rem(z + k, 8)
            forwarded = rem(turn + k + (0 if student else 2), 4) == 0
            if not student:
                relayed = jnp.logical_and(rem(turn + k + 1, 4) == 0, k != 4)
                forwarded = jnp.logical_or(forwarded, relayed)
            near = jnp.logical_or(k == 1, k == 7)

            @pl.when(jnp.logical_and(k != 0, jnp.logical_or(near, jnp.logical_not(forwarded))))
            def _():
                arrived("s0" if student else "t0", (zs if student else zt).at[row], k)

            scores(student, row, j)

        return body

    def over_x(t):
        for i in (2, 1, 3):
            send(None, f"x{t}{i}", tot.at[t], xin.at[t, i - 1], to_x[i])

    def over_z(t):
        for i in (1, 2, 3):
            arrived(f"x{t}{i}", xin.at[t, i - 1])
        xsum[t] = tot[t] + xin[t, 0] + xin[t, 1] + xin[t, 2]
        for i in (4, 3, 5, 2, 6, 1, 7):
            send(None, f"z{t}{i}", xsum.at[t], zin.at[t, i - 1], to_z[i])

    def totals(t):
        for i in range(1, 8):
            arrived(f"z{t}{i}", zin.at[t, i - 1])
        whole = xsum[t]
        for i in range(7):
            whole = whole + zin[t, i]
        factor[t] = 10.0 / whole

    lax.fori_loop(0, 6, chunk(True), None)
    relay(3)
    relay(5)
    lax.fori_loop(6, 8, chunk(True), None)
    over_x(1)
    lax.fori_loop(0, 8, chunk(False), None)
    over_x(0)
    over_z(1)

    def paired(j, _):
        row = rem(z + offset(j), 8)
        names = jnp.broadcast_to(zs[row, 192:193].astype(F32), (256, 256))
        crops = lax.broadcasted_iota(jnp.int32, (256, 256), 0).astype(F32)
        onehot = jnp.where(names == crops, 1.0, 0.0).astype(BF16)
        ag[j] = lax.dot_general(
            zs[row, 0:192], onehot, (((1,), (1,)), ((), ())), preferred_element_type=F32
        )

    lax.fori_loop(0, 8, paired, None)
    over_z(0)
    totals(1)
    for j in range(8):
        row = rows_z[ORDER[j]]
        scaled = zs[row, 0:192].astype(F32) * factor[1, pl.ds(row, 1), :]
        at[1, :, j * 256 : (j + 1) * 256] = scaled.astype(BF16)

    def term(t, m):
        return lax.dot_general(
            e_buf[pl.ds(pl.multiple_of(m * 256, 256), 256), t * 2048 : (t + 1) * 2048],
            at[t],
            (((1,), (1,)), ((), ())),
            preferred_element_type=F32,
        )

    def student_term(m, _):
        g[m] = term(1, m)

    lax.fori_loop(0, 8, student_term, None)
    totals(0)
    for j in range(8):
        row = rows_z[ORDER[j]]
        at[0, :, j * 256 : (j + 1) * 256] = (ag[j] * -factor[0, pl.ds(row, 1), :]).astype(BF16)

    def both(k, whose):
        m = ys[k] * 2 + whose
        return g[m] + term(0, m)

    def theirs(i, k):
        gs_out[i] = both(k, 1 - core)
        send(None, f"g{i}", gs_out.at[i], gs_in.at[i], sibling)

    def ours(i, k):
        part = both(k, core)
        arrived(f"g{i}", gs_in.at[i])
        part = part + gs_in[i]
        return jnp.concatenate([part, jnp.zeros((256, 64), F32)], axis=1).T[0:192]

    theirs(0, 2)
    theirs(1, 1)
    for i, k in enumerate((2, 1, 3)):
        if i == 0:
            theirs(2, 3)
        ry_out[i] = ours(i, k).astype(BF16)
        send(None, f"y{k}", ry_out.at[i], ry_in.at[k - 1], to_y[k])
    theirs(3, 0)
    total = ours(3, 0)
    for k in (2, 1, 3):
        arrived(f"y{k}", ry_in.at[k - 1])
        total = total + ry_in[k - 1].astype(F32)
    cols = sw_ref[:, half]
    norms = jnp.sqrt(jnp.sum(cols * cols, axis=0, keepdims=True) + EPS)
    unit = cols / norms
    grad_ref[...] = (total - unit * jnp.sum(unit * total, axis=0, keepdims=True)) / norms

    some = [
        zs.at[0], zt.at[0], wbuf.at[0, 0], wbuf.at[0, 0, first], cbuf.at[0], tot.at[0], gs_out.at[0],
    ]
    like = {(ref.shape, ref.dtype): ref for ref in some}
    for i, (when, shape, dtype) in enumerate(sent):
        ref = like[shape, dtype]

        def drain(i=i, ref=ref):
            pltpu.make_async_remote_copy(
                src_ref=ref, dst_ref=ref, send_sem=ssem.at[i], recv_sem=rsem.at[0], device_id=sibling, device_id_type=MESH
            ).wait_send()

        if when is None:
            drain()
        else:
            pl.when(when)(drain)


def shards(teacher_weight, student_weight, teacher_feats, student_feats, pairing, center):
    hbm = pl.BlockSpec(memory_space=pltpu.HBM)
    vmem = pl.BlockSpec(memory_space=pltpu.VMEM)
    student_grad = pl.pallas_call(
        kernel,
        out_shape=jax.ShapeDtypeStruct((192, 256), F32),
        in_specs=[hbm] * 6,
        out_specs=vmem,
        scratch_shapes=[
            pltpu.VMEM((192, 512), F32),
            pltpu.VMEM((192, 512), F32),
            pltpu.VMEM((192, 256), BF16),
            pltpu.VMEM((192, 256), BF16),
            pltpu.VMEM((1, 256), jnp.int32),
            pltpu.VMEM((128, 128), F32),
            pltpu.VMEM((4, 2, 256, 384), BF16),
            pltpu.VMEM((4, 8, 128), F32),
            pltpu.VMEM((8, 208, 256), BF16),
            pltpu.VMEM((8, 192, 256), BF16),
            pltpu.VMEM((2048, 4096), BF16),
            pltpu.VMEM((2048, 128), F32),
            pltpu.VMEM((2, 8, 256), F32),
            pltpu.VMEM((2, 3, 8, 256), F32),
            pltpu.VMEM((2, 8, 256), F32),
            pltpu.VMEM((2, 7, 8, 256), F32),
            pltpu.VMEM((2, 8, 256), F32),
            pltpu.VMEM((8, 192, 256), F32),
            pltpu.VMEM((2, 192, 2048), BF16),
            pltpu.VMEM((8, 256, 192), F32),
            pltpu.VMEM((4, 256, 192), F32),
            pltpu.VMEM((4, 256, 192), F32),
            pltpu.VMEM((3, 192, 256), BF16),
            pltpu.VMEM((3, 192, 256), BF16),
            pltpu.SemaphoreType.DMA((SENDS,)),
            pltpu.SemaphoreType.DMA((len(RECV),)),
            pltpu.SemaphoreType.DMA((LOADS,)),
        ],
        compiler_params=pltpu.CompilerParams(
            collective_id=0, has_side_effects=True, vmem_limit_bytes=60 * 1024 * 1024
        ),
    )(
        teacher_weight,
        student_weight,
        teacher_feats[0].T,
        student_feats[0].T,
        pairing,
        center.reshape(128, 128),
    )
    return 0.994 * teacher_weight + 0.006 * student_weight, student_grad


def solution(mesh):
    columns = P(None, ("proto", "fsdp"))
    return jax.shard_map(
        shards,
        mesh=mesh,
        in_specs=(columns, columns, P("dp", "fsdp", None), P("dp", "fsdp", None), P("dp", "fsdp"), P("proto")),
        out_specs=(columns, P(None, ("proto", "fsdp", "dp"))),
        check_vma=False,
    )
```

```python
import math

import jax
import jax.numpy as jnp
import numpy as np
from jax import lax
from jax.experimental import pallas as pl
from jax.experimental.pallas import tpu as pltpu
from jax.sharding import PartitionSpec as P

MESH = pl.DeviceIdType.MESH
F32, BF16 = jnp.float32, jnp.bfloat16
T_SCALE = math.log2(math.e) / 0.04
S_SCALE = math.log2(math.e) / 0.1
EPS = 1e-06


def rem(a, n):
    return lax.rem(a, np.int32(n))


def div(a, n):
    return lax.div(a, np.int32(n))


def device(x, y, z, core):
    return ((rem(x, 2) * 8 + z) * 2 + core, y, div(x, 2))


RECV = (
    [f"t{i}" for i in range(8)]
    + [f"s{i}" for i in range(8)]
    + ["wra", "wrb", "wla", "wlb", "wr2", "wl2"]
    + [f"ws{i}" for i in range(4)]
    + [f"c{i}" for i in range(1, 4)]
    + [f"x{t}{i}" for t in range(2) for i in range(1, 4)]
    + [f"z{t}{i}" for t in range(2) for i in range(1, 8)]
    + [f"g{i}" for i in range(4)]
    + [f"y{i}" for i in range(1, 4)]
)
RECV = {name: i for i, name in enumerate(RECV)}
SENDS = 128
LOADS = 6
ORDER = (0, 1, 7, 2, 6, 3, 5, 4)


def kernel(
    tw_hbm, sw_hbm, tf_hbm, sf_hbm, pair_hbm, cen_hbm, grad_ref,
    tw_ref, sw_ref, tf_ref, sf_ref, pair_ref, cen_ref,
    wbuf, cbuf, zs, zt, e_buf, cb, tot, xin, xsum, zin, factor, ag, at, g, gs_out, gs_in, ry_out, ry_in,
    ssem, rsem, lsem,
):
    f, y, d = lax.axis_index("fsdp"), lax.axis_index("proto"), lax.axis_index("dp")
    core, z = rem(f, 2), rem(div(f, 2), 8)
    x = d * 2 + div(f, 16)

    xs = [rem(x + k, 4) for k in range(4)]
    ys = [rem(y + k, 4) for k in range(4)]
    rows_z = [rem(z + k, 8) for k in range(8)]
    to_x = [device(xs[k], y, z, core) for k in range(4)]
    to_y = [device(x, ys[k], z, core) for k in range(4)]
    to_z = [device(x, y, rows_z[k], core) for k in range(8)]
    sibling = device(x, y, z, 1 - core)
    turn = rem(z + y + 8 - x, 4)
    at_turn = [turn == k for k in range(4)]

    def here(k, student):
        return at_turn[(-k + (0 if student else 2)) % 4]

    sent = []

    def send(when, name, src, dst, to):
        i = len(sent)
        pltpu.make_async_remote_copy(
            src_ref=src, dst_ref=dst, send_sem=ssem.at[i], recv_sem=rsem.at[RECV[name]], device_id=to, device_id_type=MESH
        ).start()
        sent.append((when, src.shape, src.dtype))

    def arrived(name, ref, offset=0):
        pltpu.make_async_remote_copy(
            src_ref=ref, dst_ref=ref, send_sem=ssem.at[0], recv_sem=rsem.at[RECV[name] + offset],
            device_id=sibling, device_id_type=MESH,
        ).wait_recv()

    peers = [sibling] + [to_y[k] for k in (1, 2, 3)] + [to_x[k] for k in (1, 2, 3)] + [to_z[k] for k in range(1, 8)]
    barrier = pltpu.get_barrier_semaphore()
    for peer in peers:
        pl.semaphore_signal(barrier, inc=1, device_id=peer, device_id_type=MESH)

    loads = [
        pltpu.make_async_copy(src, dst, lsem.at[i])
        for i, (src, dst) in enumerate(
            ((sf_hbm, sf_ref), (tf_hbm, tf_ref), (pair_hbm, pair_ref), (sw_hbm, sw_ref), (tw_hbm, tw_ref), (cen_hbm, cen_ref))
        )
    ]
    for load in loads:
        load.start()

    def normalized(feats_ref):
        feats = feats_ref[...].astype(F32)
        return (feats * lax.rsqrt(jnp.sum(feats * feats, axis=0, keepdims=True) + EPS)).astype(BF16)

    for load in loads[:3]:
        load.wait()

    @pl.when(here(0, True))
    def _():
        zs[z, 0:192] = normalized(sf_ref)
        zs[z, 192:208] = jnp.broadcast_to(pair_ref[...].astype(F32), (16, 256)).astype(BF16)

    @pl.when(here(0, False))
    def _():
        zt[z] = normalized(tf_ref)

    pl.semaphore_wait(barrier, len(peers))

    def block(student, k):
        return (zs if student else zt).at[rows_z[k % 8]]

    def name_of(student, k):
        return ("s" if student else "t") + str(k % 8)

    def along_x(when, student, k, steps=(2, 1, 3)):
        for i in steps:
            send(when, name_of(student, k), block(student, k), block(student, k), to_x[i])

    def along_z(when, student, steps, k=0):
        for i in steps:
            send(when, name_of(student, k - i), block(student, k), block(student, k), to_z[i])

    for student in (True, False):
        mine = here(0, student)

        @pl.when(mine)
        def _(student=student, mine=mine):
            along_x(mine, student, 0)
            along_z(mine, student, (2, 6))

    for load in loads[3:]:
        load.wait()
    half = pl.ds(pl.multiple_of(d * 256, 256), 256)
    s_cols = sw_ref[:, half]
    t_cols = 0.994 * tw_ref[:, half] + 0.006 * s_cols
    ws = s_cols * lax.rsqrt(jnp.sum(s_cols * s_cols, axis=0, keepdims=True) + EPS)
    wt = t_cols * lax.rsqrt(jnp.sum(t_cols * t_cols, axis=0, keepdims=True) + EPS)
    wbuf[y, core] = jnp.concatenate([wt, ws], axis=0).T.astype(BF16)

    lowest = jnp.min(jnp.min(cen_ref[...], axis=0, keepdims=True), axis=1, keepdims=True)
    cbuf[y, 4:5, :] = jnp.broadcast_to(lowest, (1, 128))
    for k in range(4):
        row = 4 * (f - core) + 4 * (k // 2) + 2 * d + k % 2
        cbuf[y, k : k + 1, :] = cen_ref[pl.ds(row, 1), :]
    cbuf[y, 5:8, :] = jnp.zeros((3, 128), F32)

    first, last = pl.ds(0, 128), pl.ds(128, 128)
    own = wbuf.at[y, core]
    for name, part, k in (("wra", first, 1), ("wlb", last, 3), ("wrb", last, 1), ("wla", first, 3)):
        send(None, name, own.at[part], own.at[part], to_y[k])
    for k in (1, 3, 2):
        send(None, f"c{k}", cbuf.at[y], cbuf.at[y], to_y[k])
    send(None, "ws0", own, own, sibling)

    def forward(k):
        for student in (True, False):
            mine = here(k, student)

            @pl.when(mine)
            def _(student=student, mine=mine):
                arrived(name_of(student, k), block(student, k))
                if k == 2:
                    along_z(mine, student, (7,) if student else (7, 6), k)
                if k == 6:
                    along_z(mine, student, (1, 2) if student else (1,), k)
                along_x(mine, student, k, (2, 1, 3) if student or k == 4 else (3, 1))

    def relay(k):
        mine = here(k - 1, False)

        @pl.when(mine)
        def _():
            arrived(name_of(False, k), block(False, k))
            along_x(mine, False, k, (3,))

    before, after = wbuf.at[ys[3], core], wbuf.at[ys[1], core]
    opposite = wbuf.at[ys[2], core]
    forward(2)
    forward(6)
    for student in (True,):

        @pl.when(jnp.logical_not(here(0, student)))
        def _(student=student):
            arrived(name_of(student, 0), block(student, 0))

        along_z(None, student, (1, 7))

    arrived("wra", before.at[first])
    send(None, "wr2", before.at[first], before.at[first], to_y[1])
    arrived("wlb", after.at[last])
    send(None, "wl2", after.at[last], after.at[last], to_y[3])

    for k in (1, 2, 3):
        arrived(f"c{k}", cbuf.at[ys[(4 - k) % 4]])
    floor = jnp.minimum(
        jnp.minimum(cbuf[0, 4:5, :], cbuf[1, 4:5, :]), jnp.minimum(cbuf[2, 4:5, :], cbuf[3, 4:5, :])
    )
    for k in range(16):
        row = (cbuf[k // 4, k % 4 : k % 4 + 1, :] - floor) * T_SCALE
        cb[k * 128 : (k + 1) * 128, :] = jnp.broadcast_to(row, (128, 128)).T

    forward(3)
    forward(5)
    arrived("wrb", before.at[last])
    send(None, "ws1", before, before, sibling)
    arrived("wla", after.at[first])
    send(None, "ws2", after, after, sibling)
    forward(4)
    for student in (False,):

        @pl.when(jnp.logical_not(here(0, student)))
        def _(student=student):
            arrived(name_of(student, 0), block(student, 0))

        along_z(None, student, (1, 7))

    relay(2)
    relay(6)
    arrived("wr2", opposite.at[first])
    arrived("wl2", opposite.at[last])
    send(None, "ws3", opposite, opposite, sibling)

    for i, k in ((0, 0), (1, 3), (2, 1), (3, 2)):
        arrived(f"ws{i}", wbuf.at[ys[k], 1 - core])

    def scores(student, row, j):
        pad = jnp.zeros((64, 256), BF16)
        rhs = jnp.concatenate([pad, zs[row, 0:192]] if student else [zt[row], pad], axis=0)
        lanes = pl.ds(pl.multiple_of((2048 if student else 0) + j * 256, 256), 256)
        total = jnp.zeros((8, 256), F32)
        low = 128 if student else 0
        for m in range(8):
            rows = pl.ds(m * 256, 256)
            score = jnp.dot(wbuf[m // 2, m % 2, :, low : low + 256], rhs, preferred_element_type=F32)
            if student:
                value = jnp.exp2(score * S_SCALE)
            else:
                shift = cb[rows, :]
                value = jnp.exp2(score * T_SCALE - jnp.concatenate([shift, shift], axis=1))
            e_buf[rows, lanes] = value.astype(BF16)
            total = total + jnp.sum(value.reshape(32, 8, 256), axis=0)
        tot[1 if student else 0, pl.ds(row, 1), :] = jnp.sum(total, axis=0, keepdims=True)

    def offset(j):
        step = div(j + 1, 2)
        return jnp.where(rem(j, 2) == 1, step, rem(8 - step, 8))

    def chunk(student):
        def body(j, _):
            k = offset(j)
            row = rem(z + k, 8)
            forwarded = rem(turn + k + (0 if student else 2), 4) == 0
            if not student:
                relayed = jnp.logical_and(rem(turn + k + 1, 4) == 0, k != 4)
                forwarded = jnp.logical_or(forwarded, relayed)
            near = jnp.logical_or(k == 1, k == 7)

            @pl.when(jnp.logical_and(k != 0, jnp.logical_or(near, jnp.logical_not(forwarded))))
            def _():
                arrived("s0" if student else "t0", (zs if student else zt).at[row], k)

            scores(student, row, j)

        return body

    def over_x(t):
        for i in (2, 1, 3):
            send(None, f"x{t}{i}", tot.at[t], xin.at[t, i - 1], to_x[i])

    def over_z(t):
        for i in (1, 2, 3):
            arrived(f"x{t}{i}", xin.at[t, i - 1])
        xsum[t] = tot[t] + xin[t, 0] + xin[t, 1] + xin[t, 2]
        for i in (4, 3, 5, 2, 6, 1, 7):
            send(None, f"z{t}{i}", xsum.at[t], zin.at[t, i - 1], to_z[i])

    def totals(t):
        for i in range(1, 8):
            arrived(f"z{t}{i}", zin.at[t, i - 1])
        whole = xsum[t]
        for i in range(7):
            whole = whole + zin[t, i]
        factor[t] = 10.0 / whole

    lax.fori_loop(0, 6, chunk(True), None)
    relay(3)
    relay(5)
    lax.fori_loop(6, 8, chunk(True), None)
    over_x(1)
    lax.fori_loop(0, 8, chunk(False), None)
    over_x(0)
    over_z(1)

    def paired(j, _):
        row = rem(z + offset(j), 8)
        names = jnp.broadcast_to(zs[row, 192:193].astype(F32), (256, 256))
        crops = lax.broadcasted_iota(jnp.int32, (256, 256), 0).astype(F32)
        onehot = jnp.where(names == crops, 1.0, 0.0).astype(BF16)
        ag[j] = lax.dot_general(
            zs[row, 0:192], onehot, (((1,), (1,)), ((), ())), preferred_element_type=F32
        )

    lax.fori_loop(0, 8, paired, None)
    over_z(0)
    totals(1)
    for j in range(8):
        row = rows_z[ORDER[j]]
        scaled = zs[row, 0:192].astype(F32) * factor[1, pl.ds(row, 1), :]
        at[1, :, j * 256 : (j + 1) * 256] = scaled.astype(BF16)

    def term(t, m):
        return lax.dot_general(
            e_buf[pl.ds(pl.multiple_of(m * 256, 256), 256), t * 2048 : (t + 1) * 2048],
            at[t],
            (((1,), (1,)), ((), ())),
            preferred_element_type=F32,
        )

    def student_term(m, _):
        g[m] = term(1, m)

    lax.fori_loop(0, 8, student_term, None)
    totals(0)
    for j in range(8):
        row = rows_z[ORDER[j]]
        at[0, :, j * 256 : (j + 1) * 256] = (ag[j] * -factor[0, pl.ds(row, 1), :]).astype(BF16)

    def both(k, whose):
        m = ys[k] * 2 + whose
        return g[m] + term(0, m)

    def theirs(i, k):
        gs_out[i] = both(k, 1 - core)
        send(None, f"g{i}", gs_out.at[i], gs_in.at[i], sibling)

    def ours(i, k):
        part = both(k, core)
        arrived(f"g{i}", gs_in.at[i])
        part = part + gs_in[i]
        return jnp.concatenate([part, jnp.zeros((256, 64), F32)], axis=1).T[0:192]

    theirs(0, 2)
    theirs(1, 1)
    for i, k in enumerate((2, 1, 3)):
        if i == 0:
            theirs(2, 3)
        ry_out[i] = ours(i, k).astype(BF16)
        send(None, f"y{k}", ry_out.at[i], ry_in.at[k - 1], to_y[k])
    theirs(3, 0)
    total = ours(3, 0)
    for k in (2, 1, 3):
        arrived(f"y{k}", ry_in.at[k - 1])
        total = total + ry_in[k - 1].astype(F32)
    cols = sw_ref[:, half]
    norms = jnp.sqrt(jnp.sum(cols * cols, axis=0, keepdims=True) + EPS)
    unit = cols / norms
    grad_ref[...] = (total - unit * jnp.sum(unit * total, axis=0, keepdims=True)) / norms

    some = [
        zs.at[0], zt.at[0], wbuf.at[0, 0], wbuf.at[0, 0, first], cbuf.at[0], tot.at[0], gs_out.at[0],
    ]
    like = {(ref.shape, ref.dtype): ref for ref in some}
    for i, (when, shape, dtype) in enumerate(sent):
        ref = like[shape, dtype]

        def drain(i=i, ref=ref):
            pltpu.make_async_remote_copy(
                src_ref=ref, dst_ref=ref, send_sem=ssem.at[i], recv_sem=rsem.at[0], device_id=sibling, device_id_type=MESH
            ).wait_send()

        if when is None:
            drain()
        else:
            pl.when(when)(drain)


def shards(teacher_weight, student_weight, teacher_feats, student_feats, pairing, center):
    hbm = pl.BlockSpec(memory_space=pltpu.HBM)
    vmem = pl.BlockSpec(memory_space=pltpu.VMEM)
    student_grad = pl.pallas_call(
        kernel,
        out_shape=jax.ShapeDtypeStruct((192, 256), F32),
        in_specs=[hbm] * 6,
        out_specs=vmem,
        scratch_shapes=[
            pltpu.VMEM((192, 512), F32),
            pltpu.VMEM((192, 512), F32),
            pltpu.VMEM((192, 256), BF16),
            pltpu.VMEM((192, 256), BF16),
            pltpu.VMEM((1, 256), jnp.int32),
            pltpu.VMEM((128, 128), F32),
            pltpu.VMEM((4, 2, 256, 384), BF16),
            pltpu.VMEM((4, 8, 128), F32),
            pltpu.VMEM((8, 208, 256), BF16),
            pltpu.VMEM((8, 192, 256), BF16),
            pltpu.VMEM((2048, 4096), BF16),
            pltpu.VMEM((2048, 128), F32),
            pltpu.VMEM((2, 8, 256), F32),
            pltpu.VMEM((2, 3, 8, 256), F32),
            pltpu.VMEM((2, 8, 256), F32),
            pltpu.VMEM((2, 7, 8, 256), F32),
            pltpu.VMEM((2, 8, 256), F32),
            pltpu.VMEM((8, 192, 256), F32),
            pltpu.VMEM((2, 192, 2048), BF16),
            pltpu.VMEM((8, 256, 192), F32),
            pltpu.VMEM((4, 256, 192), F32),
            pltpu.VMEM((4, 256, 192), F32),
            pltpu.VMEM((3, 192, 256), BF16),
            pltpu.VMEM((3, 192, 256), BF16),
            pltpu.SemaphoreType.DMA((SENDS,)),
            pltpu.SemaphoreType.DMA((len(RECV),)),
            pltpu.SemaphoreType.DMA((LOADS,)),
        ],
        compiler_params=pltpu.CompilerParams(
            collective_id=0, has_side_effects=True, vmem_limit_bytes=60 * 1024 * 1024
        ),
    )(
        teacher_weight,
        student_weight,
        teacher_feats[0].T,
        student_feats[0].T,
        pairing,
        center.reshape(128, 128),
    )
    return 0.994 * teacher_weight + 0.006 * student_weight, student_grad


def solution(mesh):
    columns = P(None, ("proto", "fsdp"))
    return jax.shard_map(
        shards,
        mesh=mesh,
        in_specs=(columns, columns, P("dp", "fsdp", None), P("dp", "fsdp", None), P("dp", "fsdp"), P("proto")),
        out_specs=(columns, P(None, ("proto", "fsdp", "dp"))),
        check_vma=False,
    )
```
